256 devices in a mesh: patch: 16 (over z, x_hi), sub: 16 (over x_lo, y, core).
Axes of the slice: x: 4 (x_hi: 2, x_lo: 2; x = x_hi * 2 + x_lo), y: 4, z: 8, core: 2. Of those that a mesh axis runs over, the one named last changes fastest.
Arguments:
- displacement: float32 [3, 128, 32768], P(None, 'patch', 'sub'), may hold values from -3 to 3
- load: float32 [3, 128, 32768], P(None, 'patch', 'sub'), may hold values from -6 to 6
- foundation: float32 [3, 128, 32768], P(None, 'patch', 'sub'), may hold values from 0.2 to 2
- layup: int32 [128, 32768], P('patch', 'sub'), may hold values from 0 to 7
- layup_stiffness: float32 [8, 6, 6], replicated, as said below
- w_first: bfloat16 [128, 6], replicated, may hold values from -2.5 to 2.5
- w_mid: bfloat16 [3, 128, 128], replicated, may hold values from -0.5 to 0.5
- w_last: bfloat16 [6, 128], replicated, may hold values from -0.5 to 0.5
Outputs:
- residual: float32 [3, 128, 32768], P(None, 'patch', 'sub')
- adjoint: float32 [3, 128, 32768], P(None, 'patch', 'sub')
- grad_first: float32 [128, 6], replicated
- grad_mid: float32 [3, 128, 128], replicated
- grad_last: float32 [6, 128], replicated
The draws below stay inside these ranges and needn't reach their ends.
Inputs may be any that keep to these rules, and one draw needn't show every extreme that they name: `layup_stiffness`: each of the 8 matrices is symmetric positive definite.
All inputs are finite; a program needn't handle non-finite values.
Results may differ from the reference program's by a relative error of at most 0.0006.
The reference program's roundings to bfloat16 on the way count: a program that leaves them out, or rounds other values in their place, can miss the bound.
Values sent between devices are 32-bit elements; how exact they have to be, the bound alone decides.
A program may use at most 128 MiB of HBM per device.

```python
import math
import jax
import jax.numpy as jnp
from jax import lax

H = 128
MID = 3
NL = 8
ITERS = 4
NX = 128
NY = 32768


def draw_layup_stiffness(key, part):
    first_key, second_key = jax.random.split(jax.random.fold_in(key, 17))
    mixing = jax.random.normal(first_key, (NL, 6, 6), jnp.float32) * 0.9
    diagonal = jax.random.uniform(second_key, (NL, 6), jnp.float32, 1.0, 3.0)
    coupling = jnp.einsum('lab,lcb->lac', mixing, mixing) / 6.0
    return coupling + diagonal[:, :, None] * jnp.eye(6, dtype=jnp.float32)


def touch_ends(values, key, low, top_value):
    longest = values.shape.index(max(values.shape))
    spots = []
    for shift in (0, 1):
        where = [jax.random.randint(jax.random.fold_in(key, axis), (), 0, length) for axis, length in enumerate(values.shape)]
        where[longest] = (where[longest] + shift) % values.shape[longest]
        spots.append(tuple(where))
    return values.at[spots[0]].set(low).at[spots[1]].set(top_value)


def shard_levels(key, dims, pieces, low, top_value):
    level, own = 1.0, jax.random.fold_in(key, 6)
    for position, parts in pieces:
        draws = jnp.exp(jax.random.uniform(jax.random.fold_in(own, position), (parts,), jnp.float32, low / len(pieces), top_value / len(pieces)))
        level = level * jnp.repeat(draws, dims[position] // parts).reshape([-1 if axis == position else 1 for axis in range(len(dims))])
    return level


def bell_draw(rng, extent, width, limit, shards=(), kind=jnp.bfloat16):
    loudness = shard_levels(rng, extent, shards, -0.22, 0.18) if shards else 1.0
    array = jax.random.normal(rng, extent, jnp.float32) * width * loudness
    return jnp.minimum(jnp.maximum(array, -limit), limit).astype(kind)


def setup_inputs(seed: int = 0) -> dict:
    arg_keys = jax.random.split(jax.random.key(seed), 9)
    return {
        "displacement": bell_draw(arg_keys[0], (3, NX, NY), 0.4, 3.0, ((1, 16), (2, 16)), jnp.float32),
        "load": bell_draw(arg_keys[1], (3, NX, NY), 1.0, 6.0, ((1, 16), (2, 16)), jnp.float32),
        "foundation": jnp.clip(jnp.exp(math.log(2.0) - 2.3025851 * jax.random.uniform(arg_keys[2], (3, NX, NY), jnp.float32) ** shard_levels(arg_keys[2], (3, NX, NY), ((1, 16), (2, 16)), -0.2, 0.2)), 0.2, 2.0),
        "layup": touch_ends(jax.random.randint(arg_keys[3], (NX, NY), 0, NL), jax.random.fold_in(arg_keys[3], 1), 0, NL - 1).astype(jnp.int32),
        "layup_stiffness": draw_layup_stiffness(jax.random.fold_in(arg_keys[8], 71), 0),
        "w_first": bell_draw(arg_keys[5], (H, 6), 6 ** -0.5, 2.5),
        "w_mid": bell_draw(arg_keys[6], (MID, H, H), H ** -0.5, 0.5),
        "w_last": bell_draw(arg_keys[7], (6, H), H ** -0.5, 0.5),
    }


BASIS_VALUE = (0.125, 0.75, 0.125)
BASIS_SLOPE = (-0.5, 0.0, 0.5)
BASIS_CURVE = (1.0, -2.0, 1.0)
HOOP_CURVATURE = 0.25


def correlate(padded, along_x, along_y):
    row_count = padded.shape[-2] - 2
    col_count = padded.shape[-1] - 2
    partial_x = None
    for offset in range(3):
        if along_x[offset] != 0.0:
            weighted = along_x[offset] * padded[..., offset:offset + row_count, :]
            partial_x = weighted if partial_x is None else partial_x + weighted
    running = None
    for offset in range(3):
        if along_y[offset] != 0.0:
            weighted = along_y[offset] * partial_x[..., offset:offset + col_count]
            running = weighted if running is None else running + weighted
    return running


def mirrored(padded, along_x, along_y):
    return correlate(padded, along_x[::-1], along_y[::-1])


def strains(padded):
    along_u, along_v, along_w = padded[0], padded[1], padded[2]
    return jnp.stack([
        correlate(along_u, BASIS_SLOPE, BASIS_VALUE),
        correlate(along_v, BASIS_VALUE, BASIS_SLOPE) + HOOP_CURVATURE * correlate(along_w, BASIS_VALUE, BASIS_VALUE),
        correlate(along_u, BASIS_VALUE, BASIS_SLOPE) + correlate(along_v, BASIS_SLOPE, BASIS_VALUE),
        -correlate(along_w, BASIS_CURVE, BASIS_VALUE),
        -correlate(along_w, BASIS_VALUE, BASIS_CURVE),
        -2.0 * correlate(along_w, BASIS_SLOPE, BASIS_SLOPE)])


def forces(spread):
    force_u = mirrored(spread[0], BASIS_SLOPE, BASIS_VALUE) + mirrored(spread[2], BASIS_VALUE, BASIS_SLOPE)
    force_v = mirrored(spread[1], BASIS_VALUE, BASIS_SLOPE) + mirrored(spread[2], BASIS_SLOPE, BASIS_VALUE)
    force_w = (HOOP_CURVATURE * mirrored(spread[1], BASIS_VALUE, BASIS_VALUE)
               - mirrored(spread[3], BASIS_CURVE, BASIS_VALUE)
               - mirrored(spread[4], BASIS_VALUE, BASIS_CURVE)
               - 2.0 * mirrored(spread[5], BASIS_SLOPE, BASIS_SLOPE))
    return jnp.stack([force_u, force_v, force_w])


def apply_layup(stiffness_map, strain):
    running = stiffness_map[:, 0] * strain[0]
    for column in range(1, 6):
        running = running + stiffness_map[:, column] * strain[column]
    return running


def outer_product(left, right):
    return lax.dot_general(left, right, (((1,), (1,)), ((), ())), preferred_element_type=jnp.float32)


def forward_mlp(inputs, w_first, w_mid, w_last):
    hidden_layer = jnp.tanh(jnp.dot(w_first, inputs, preferred_element_type=jnp.float32)).astype(jnp.bfloat16)
    activations = [hidden_layer]
    for layer_index in range(w_mid.shape[0]):
        hidden_layer = jnp.tanh(jnp.dot(w_mid[layer_index], hidden_layer, preferred_element_type=jnp.float32)).astype(jnp.bfloat16)
        activations.append(hidden_layer)
    return jnp.dot(w_last, hidden_layer, preferred_element_type=jnp.float32), activations


def backward_mlp(inputs, activations, upstream, w_mid, w_last):
    grad_last = outer_product(upstream, activations[-1])
    signal = jnp.dot(w_last.T, upstream, preferred_element_type=jnp.float32)
    derivative = (signal * (1.0 - jnp.square(activations[-1].astype(jnp.float32)))).astype(jnp.bfloat16)
    mid_grads = []
    for layer_index in range(w_mid.shape[0] - 1, -1, -1):
        mid_grads.append(outer_product(derivative, activations[layer_index]))
        signal = jnp.dot(w_mid[layer_index].T, derivative, preferred_element_type=jnp.float32)
        derivative = (signal * (1.0 - jnp.square(activations[layer_index].astype(jnp.float32)))).astype(jnp.bfloat16)
    grad_first = outer_product(derivative, inputs)
    return grad_first, jnp.stack(mid_grads[::-1]), grad_last


def periodic(field, rim_width):
    return jnp.pad(field, ((0, 0), (rim_width, rim_width), (rim_width, rim_width)), mode="wrap")


def reference(displacement, load, foundation, layup, layup_stiffness, w_first, w_mid, w_last):
    def material(strain):
        result = jnp.zeros_like(strain)
        for layup_index in range(NL):
            mixed = apply_layup(layup_stiffness[layup_index][:, :, None, None], strain)
            result = jnp.where(layup[None] == layup_index, mixed, result)
        return result

    strain = strains(periodic(displacement, 1))
    inputs = strain.astype(jnp.bfloat16)
    by_row = jnp.moveaxis(inputs, 1, 0)

    def learned_row(row_inputs):
        outcome, activations = forward_mlp(row_inputs, w_first, w_mid, w_last)
        return outcome

    learned = jnp.moveaxis(lax.map(learned_row, by_row), 0, 1)
    stress = material(strain) + learned
    residual = forces(periodic(stress, 1)) + foundation * displacement - load

    def operate(search):
        return forces(periodic(material(strains(periodic(search, 1))), 1)) + foundation * search

    adjoint = jnp.zeros_like(residual)
    remainder = residual
    direction = residual
    norm_now = jnp.sum(remainder * remainder)
    for step_index in range(ITERS):
        mapped = operate(direction)
        step_size = norm_now / jnp.sum(direction * mapped)
        adjoint = adjoint + step_size * direction
        remainder = remainder - step_size * mapped
        norm_next = jnp.sum(remainder * remainder)
        direction = remainder + (norm_next / norm_now) * direction
        norm_now = norm_next

    upstream = strains(periodic(adjoint, 1)).astype(jnp.bfloat16)

    def accumulate(running, row_pair):
        row_inputs, row_upstream = row_pair
        outcome, activations = forward_mlp(row_inputs, w_first, w_mid, w_last)
        gradients = backward_mlp(row_inputs, activations, row_upstream, w_mid, w_last)
        return jax.tree.map(jnp.add, running, gradients), None

    start = (jnp.zeros((H, 6), jnp.float32), jnp.zeros((MID, H, H), jnp.float32), jnp.zeros((6, H), jnp.float32))
    totals, unused = lax.scan(accumulate, start, (by_row, jnp.moveaxis(upstream, 1, 0)))
    return residual, adjoint, totals[0], totals[1], totals[2]
```

```python
import functools

import jax
import jax.numpy as jnp
from jax import lax
from jax.experimental import pallas as pl
from jax.experimental.pallas import tpu as pltpu
from jax.sharding import PartitionSpec as P

ITERS = 4
PATCH_SUB = ("patch", "sub")
PATCH = "patch"
SUB = "sub"


BASIS_VALUE = (0.125, 0.75, 0.125)
BASIS_SLOPE = (-0.5, 0.0, 0.5)
BASIS_CURVE = (1.0, -2.0, 1.0)
HOOP_CURVATURE = 0.25


def by_axis(value, axes):
    return lax.psum(value, axes)


def padded_2(cells, sides, width):
    for axis, dim in sides:
        count = lax.axis_size(axis)
        head = lax.slice_in_dim(cells, 0, width, axis=dim)
        tail = lax.slice_in_dim(cells, cells.shape[dim] - width, cells.shape[dim], axis=dim)
        cells = jnp.concatenate(
            [
                lax.ppermute(tail, axis, [(i, (i + 1) % count) for i in range(count)]),
                cells,
                lax.ppermute(head, axis, [((i + 1) % count, i) for i in range(count)]),
            ],
            axis=dim,
        )
    return cells


def split_up(value, dim, size):
    lengths = value.shape
    pieces = value.reshape(*lengths[:dim], size, lengths[dim] // size, *lengths[dim + 1 :])
    return jnp.moveaxis(pieces, dim, 0)


def sent_and_summed(value, axis, dim):
    size = lax.axis_size(axis)
    pieces = lax.all_to_all(split_up(value, dim, size), axis, 0, 0, tiled=True)
    return jnp.sum(pieces, axis=0)


def sent_to_all(value, axis):
    size = lax.axis_size(axis)
    return lax.all_to_all(
        jnp.broadcast_to(value[None], (size, *value.shape)), axis, 0, 0, tiled=True
    )


def of_everyone(value, axis):
    return sent_to_all(value, axis).sum(axis=0)


def packed_total(arrays, axis):
    vector, at, done = (jnp.concatenate([a.reshape(-1) for a in arrays]), 0, [])
    subtotal = of_everyone(vector, axis)
    for a in arrays:
        done.append(subtotal[at : at + a.size].reshape(a.shape))
        at += a.size
    return tuple(done)


def turned_gather(arrays, axis, dims):
    turned = [jnp.moveaxis(a, dim, 0) for a, dim in zip(arrays, dims)]
    both = jnp.concatenate([t.reshape(len(t), -1) for t in turned], axis=1)
    filled, at, done = (lax.all_gather(both, axis, axis=0, tiled=True), 0, [])
    for t, dim in zip(turned, dims):
        section = filled[:, at : at + t[0].size].reshape(-1, *t.shape[1:])
        done.append(jnp.moveaxis(section, 0, dim))
        at += t[0].size
    return tuple(done)


def correlate(padded, along_x, along_y):
    row_count = padded.shape[-2] - 2
    col_count = padded.shape[-1] - 2
    partial_x = None
    for offset in range(3):
        if along_x[offset] != 0.0:
            weighted = along_x[offset] * padded[..., offset : offset + row_count, :]
            partial_x = weighted if partial_x is None else partial_x + weighted
    running = None
    for offset in range(3):
        if along_y[offset] != 0.0:
            weighted = along_y[offset] * partial_x[..., offset : offset + col_count]
            running = weighted if running is None else running + weighted
    return running


def mirrored(padded, along_x, along_y):
    return correlate(padded, along_x[::-1], along_y[::-1])


def strains(padded):
    along_u, along_v, along_w = (padded[0], padded[1], padded[2])
    return jnp.stack(
        [
            correlate(along_u, BASIS_SLOPE, BASIS_VALUE),
            correlate(along_v, BASIS_VALUE, BASIS_SLOPE)
            + HOOP_CURVATURE * correlate(along_w, BASIS_VALUE, BASIS_VALUE),
            correlate(along_u, BASIS_VALUE, BASIS_SLOPE)
            + correlate(along_v, BASIS_SLOPE, BASIS_VALUE),
            -correlate(along_w, BASIS_CURVE, BASIS_VALUE),
            -correlate(along_w, BASIS_VALUE, BASIS_CURVE),
            -2.0 * correlate(along_w, BASIS_SLOPE, BASIS_SLOPE),
        ]
    )


def forces(spread):
    force_u = mirrored(spread[0], BASIS_SLOPE, BASIS_VALUE) + mirrored(
        spread[2], BASIS_VALUE, BASIS_SLOPE
    )
    force_v = mirrored(spread[1], BASIS_VALUE, BASIS_SLOPE) + mirrored(
        spread[2], BASIS_SLOPE, BASIS_VALUE
    )
    force_w = (
        HOOP_CURVATURE * mirrored(spread[1], BASIS_VALUE, BASIS_VALUE)
        - mirrored(spread[3], BASIS_CURVE, BASIS_VALUE)
        - mirrored(spread[4], BASIS_VALUE, BASIS_CURVE)
        - 2.0 * mirrored(spread[5], BASIS_SLOPE, BASIS_SLOPE)
    )
    return jnp.stack([force_u, force_v, force_w])


def apply_layup(stiffness_map, strain):
    running = stiffness_map[:, 0] * strain[0]
    for column in range(1, 6):
        running = running + stiffness_map[:, column] * strain[column]
    return running


def outer_product(left, right):
    return lax.dot_general(
        left, right, (((1,), (1,)), ((), ())), preferred_element_type=jnp.float32
    )


def forward_mlp(inputs, w_first, w_mid, w_last):
    hidden_layer = jnp.tanh(jnp.dot(w_first, inputs, preferred_element_type=jnp.float32)).astype(
        jnp.bfloat16
    )
    activations = [hidden_layer]
    for layer_index in range(w_mid.shape[0]):
        hidden_layer = jnp.tanh(
            jnp.dot(w_mid[layer_index], hidden_layer, preferred_element_type=jnp.float32)
        ).astype(jnp.bfloat16)
        activations.append(hidden_layer)
    return (jnp.dot(w_last, hidden_layer, preferred_element_type=jnp.float32), activations)


def backward_mlp(inputs, activations, upstream, w_mid, w_last):
    grad_last = outer_product(upstream, activations[-1])
    signal = jnp.dot(w_last.T, upstream, preferred_element_type=jnp.float32)
    derivative = (signal * (1.0 - jnp.square(activations[-1].astype(jnp.float32)))).astype(
        jnp.bfloat16
    )
    mid_grads = []
    for layer_index in range(w_mid.shape[0] - 1, -1, -1):
        mid_grads.append(outer_product(derivative, activations[layer_index]))
        signal = jnp.dot(w_mid[layer_index].T, derivative, preferred_element_type=jnp.float32)
        derivative = (
            signal * (1.0 - jnp.square(activations[layer_index].astype(jnp.float32)))
        ).astype(jnp.bfloat16)
    grad_first = outer_product(derivative, inputs)
    return (grad_first, jnp.stack(mid_grads[::-1]), grad_last)


def two_products(remainder, mapped):
    return (
        by_axis(jnp.sum(remainder * remainder), PATCH_SUB),
        by_axis(jnp.sum(remainder * mapped), PATCH_SUB),
    )


def careful(displacement, load, foundation, layup, layup_stiffness, w_first, w_mid, w_last):
    layup_count = layup_stiffness.shape[0]

    def coefficients(layup_ids):
        onehot = (
            layup_ids[None] == jnp.arange(layup_count, dtype=jnp.int32)[:, None, None]
        ).astype(jnp.float32)
        return jnp.einsum("lab,lxy->abxy", layup_stiffness, onehot, precision=lax.Precision.HIGHEST)

    stiffness_map = coefficients(layup)
    wide_ids = padded_2(layup, ((PATCH, 0), (SUB, 1)), 1)
    stiffness_wide = coefficients(wide_ids)

    def operate(search):
        padded = padded_2(search, ((PATCH, 1), (SUB, 2)), 2)
        return forces(apply_layup(stiffness_wide, strains(padded))) + foundation * search

    padded = padded_2(displacement, ((PATCH, 1), (SUB, 2)), 1)
    strain = strains(padded)
    inputs = strain.reshape(6, -1).astype(jnp.bfloat16)
    learned, activations = forward_mlp(inputs, w_first, w_mid, w_last)
    stress = apply_layup(stiffness_map, strain) + learned.reshape(strain.shape)
    spread = padded_2(stress, ((PATCH, 1), (SUB, 2)), 1)
    residual = forces(spread) + foundation * displacement - load
    adjoint = jnp.zeros_like(residual)
    remainder = residual
    mapped = operate(remainder)
    norm_now, curved = two_products(remainder, mapped)
    step_size = norm_now / curved
    direction, mapped_dir = (remainder, mapped)
    for step_index in range(ITERS):
        adjoint = adjoint + step_size * direction
        remainder = remainder - step_size * mapped_dir
        if step_index + 1 < ITERS:
            mapped = operate(remainder)
            norm_next, curved = two_products(remainder, mapped)
            beta_ratio = norm_next / norm_now
            step_size = norm_next / (curved - beta_ratio * norm_next / step_size)
            direction = remainder + beta_ratio * direction
            mapped_dir = mapped + beta_ratio * mapped_dir
            norm_now = norm_next
    cycle = padded_2(adjoint, ((PATCH, 1), (SUB, 2)), 1)
    upstream = strains(cycle).reshape(6, -1).astype(jnp.bfloat16)
    grad_first, grad_mid, grad_last = backward_mlp(inputs, activations, upstream, w_mid, w_last)
    shares = (
        sent_and_summed(grad_first, SUB, 0),
        sent_and_summed(grad_mid, SUB, 1),
        sent_and_summed(grad_last, SUB, 1),
    )
    crossed = packed_total((shares[0], shares[1], shares[2]), PATCH)
    totals = turned_gather((crossed[0], crossed[1], crossed[2]), SUB, (0, 1, 1))
    return (residual, adjoint, totals[0], totals[1], totals[2])


ROWS = 24
SEGS = 24
LANES = 128
OWN = 8
TILES = 16
STEP = 512
TRUST = 400.0
MESH = pl.DeviceIdType.MESH
PAIRS = [(a, b) for a in range(6) for b in range(a, 6)]
SPOT = {pair: k for k, pair in enumerate(PAIRS)}


def flat(ref):
    lead, mid, lanes = ref.shape
    return ref.reshape(lead * mid, lanes)


def column(ref, fields, field, row, segment):
    return flat(ref).at[pl.ds((row * fields + field) * SEGS + segment, 8, stride=fields * SEGS), :]


def lane_of():
    return lax.broadcasted_iota(jnp.int32, (SEGS, LANES), 1)


def after(field, lane):
    turned = pltpu.roll(field, LANES - 1, 1)
    return jnp.where(lane == LANES - 1, pltpu.roll(turned, SEGS - 1, 0), turned)


def before(field, lane):
    turned = pltpu.roll(field, 1, 1)
    return jnp.where(lane == 0, pltpu.roll(turned, 1, 0), turned)


def along_columns(read, y_ref, first, last):
    lane = lane_of()

    def body(e, carry):
        u, v, w = read(e)
        at = e * 7
        for k, field in enumerate((u, v, w)):
            ahead, behind = after(field, lane), before(field, lane)
            both = ahead + behind
            y_ref[at + 2 * k] = 0.75 * field + 0.125 * both
            y_ref[at + 2 * k + 1] = 0.5 * (ahead - behind)
            if k == 2:
                y_ref[at + 6] = both - 2.0 * field
        return carry

    lax.fori_loop(first, last, body, 0, unroll=2)


def strains_at(y_ref, e):
    at = e * 7

    def three(k):
        return y_ref[at - 7 + k], y_ref[at + k], y_ref[at + 7 + k]

    def value(k):
        m, c, p = three(k)
        return 0.75 * c + 0.125 * (p + m)

    def slope(k):
        return 0.5 * (y_ref[at + 7 + k] - y_ref[at - 7 + k])

    m, c, p = three(4)
    pair = p + m
    return [
        slope(0),
        value(3) + HOOP_CURVATURE * (0.75 * c + 0.125 * pair),
        value(1) + slope(2),
        2.0 * c - pair,
        -value(6),
        y_ref[at - 7 + 5] - y_ref[at + 7 + 5],
    ]


def laminate(c_ref, e, strain):
    at = e * 21
    total = [None] * 6
    for (a, b), k in SPOT.items():
        c = c_ref[at + k]
        term = c * strain[b]
        total[a] = term if total[a] is None else total[a] + term
        if a != b:
            term = c * strain[a]
            total[b] = term if total[b] is None else total[b] + term
    return total


def forces_at(s_ref, e, lane):
    at = e * 6

    def three(k):
        return s_ref[at - 6 + k], s_ref[at + k], s_ref[at + 6 + k]

    def value(k):
        m, c, p = three(k)
        return 0.75 * c + 0.125 * (p + m)

    def slope(k):
        return 0.5 * (s_ref[at - 6 + k] - s_ref[at + 6 + k])

    def spread(here, behind, ahead):
        return here + before(behind, lane) + after(ahead, lane)

    a, b = slope(0), value(2)
    force_u = spread(0.75 * a, 0.125 * a + 0.5 * b, 0.125 * a - 0.5 * b)
    a, b = slope(2), value(1)
    force_v = spread(0.75 * a, 0.125 * a + 0.5 * b, 0.125 * a - 0.5 * b)
    m, c, p = three(3)
    a = HOOP_CURVATURE * b - ((m + p) - 2.0 * c)
    d = value(4)
    half = slope(5)
    base = 0.125 * a - d
    force_w = spread(0.75 * a + 2.0 * d, base - half, base + half)
    return force_u, force_v, force_w


def fused(
    disp, load, found, lay, stiff, w1, wm, wl,
    res_o, adj_o, gf_o, gm_o, gl_o, trust_o,
    dsp, aux, lod, edge_a, edge_c, got_a, got_c, y_ref, s_ref, c_ref, x_ref, l_ref, u_ref, h_ref,
    v0, v1, v2, v3, wmt, acc_m, acc_s,
    d_out, d_in, d_mid, d_in2, e_out, e_in, e_mid, e_in2, e_end, e_in3,
    a_s, a_r, c_s, c_r, d1_s, d1_r, d2_s, d2_r, e1_s, e1_r, e2_s, e2_r, e3_s, e3_r,
):
    me_p, me_s = lax.axis_index("patch"), lax.axis_index("sub")
    count_p, count_s = lax.axis_size("patch"), lax.axis_size("sub")

    def place(dp, ds):
        return {"patch": lax.rem(me_p + dp, count_p), "sub": lax.rem(me_s + ds, count_s)}

    up, down = count_p - 1, 1
    left, right = count_s - 1, 1
    greeted = [(0, k) for k in range(1, count_s)] + [(k, 0) for k in range(1, count_p)]
    greeted += [(a, b) for a in (up, down) for b in (left, right)]
    barrier = pltpu.get_barrier_semaphore()
    for dp, ds in greeted:
        pl.semaphore_signal(barrier, inc=1, device_id=place(dp, ds), device_id_type=MESH)

    for t in range(TILES):
        cut = pl.ds(t * LANES, LANES)
        for f in range(3):
            column(dsp, 3, f, OWN, 8 + t)[...] = disp[f, :, cut]
    ends = ((0, pl.ds(0, LANES)), (1, pl.ds((TILES - 1) * LANES, LANES)))
    for side, cut in ends:
        for f in range(3):
            edge_a[side, f] = disp[f, :, cut]
            edge_a[side, 3 + f] = found[f, :, cut]
        edge_a[side, 6] = lay[:, cut].astype(jnp.float32)

    pl.semaphore_wait(barrier, len(greeted))

    def send(src, dst, sent, received, to):
        return pltpu.make_async_remote_copy(
            src_ref=src, dst_ref=dst, send_sem=sent, recv_sem=received, device_id=to, device_id_type=MESH
        )

    def rows_to(ref, fields, n, sent, received, first):
        own = pl.ds(OWN, TILES)
        below = send(
            ref.at[pl.ds((16 - n) * fields, n * fields), own, :],
            ref.at[pl.ds((8 - n) * fields, n * fields), own, :],
            sent.at[first], received.at[first], place(down, 0),
        )
        above = send(
            ref.at[pl.ds(8 * fields, n * fields), own, :],
            ref.at[pl.ds(16 * fields, n * fields), own, :],
            sent.at[first + 1], received.at[first + 1], place(up, 0),
        )
        return [below, above]

    heading = ((0, right, 1), (0, left, 0), (down, right, 1), (down, left, 0), (up, right, 1), (up, left, 0))

    def edges_to(edge, got, sent, received, first):
        return [
            send(edge.at[side], got.at[k], sent.at[first + k], received.at[first + k], place(dp, ds))
            for k, (dp, ds, side) in enumerate(heading)
        ]

    def start(copies):
        for copy in copies:
            copy.start()

    landing = ((7, 8), (0, 8), (7, 0), (0, 0), (7, 16), (0, 16))

    first_a = rows_to(dsp, 3, 2, a_s, a_r, 0) + edges_to(edge_a, got_a, a_s, a_r, 2)
    start(first_a)
    for t in range(TILES):
        cut = pl.ds(t * LANES, LANES)
        for f in range(3):
            column(aux, 4, f, OWN, 8 + t)[...] = found[f, :, cut]
        column(aux, 4, 3, OWN, 8 + t)[...] = lay[:, cut].astype(jnp.float32)
    second_a = rows_to(aux, 4, 6, a_s, a_r, 8)
    start(second_a)
    for t in range(TILES):
        cut = pl.ds(t * LANES, LANES)
        for f in range(3):
            column(lod, 3, f, 0, 8 + t)[...] = load[f, :, cut]
    for k in range(3):
        wmt[k] = wm[k].T

    for copy in first_a:
        copy.wait()
    for k, (segment, row) in enumerate(landing):
        for f in range(3):
            column(dsp, 3, f, row, segment)[...] = got_a[k, f]
            column(aux, 4, f, row, segment)[...] = got_a[k, 3 + f]
        column(aux, 4, 3, row, segment)[...] = got_a[k, 6]

    lane = lane_of()
    along_columns(lambda e: [dsp[e * 3 + f] for f in range(3)], y_ref, 6, 18)

    def strain_row(r, carry):
        e = r + 7
        strain = strains_at(y_ref, e)
        for k in range(6):
            s_ref[e * 6 + k] = strain[k]
            flat(x_ref)[pl.ds(r * (SEGS * 8) + k, SEGS, stride=8), :] = strain[k]
        return carry

    lax.fori_loop(0, 10, strain_row, 0)
    tile_lane = lax.broadcasted_iota(jnp.int32, (8, LANES), 1)
    for r in range(10):
        x_ref[10 * SEGS + 8 + r] = jnp.where(tile_lane < 64, x_ref[r * SEGS], x_ref[r * SEGS + 7])
    for r in range(10, 16):
        x_ref[10 * SEGS + 8 + r] = jnp.zeros((8, LANES), jnp.float32)

    def operand(ref, r, c):
        at = r * SEGS + 8 + c * (STEP // LANES)
        tiles = [ref[at + q] for q in range(STEP // LANES)]
        return jnp.concatenate(tiles, axis=1)[:6].astype(jnp.bfloat16)

    def learn_row(r, carry):
        slot = jnp.where((r >= 1) & (r <= 8), r - 1, 8) * 4
        for c in range(2048 // STEP):
            cut = pl.ds(c * STEP, STEP)
            hidden = jnp.tanh(
                jnp.dot(w1[...], operand(x_ref, r, c), preferred_element_type=jnp.float32)
            ).astype(jnp.bfloat16)
            h_ref[slot, :, cut] = hidden
            for k in range(3):
                hidden = jnp.tanh(
                    jnp.dot(wm[k], hidden, preferred_element_type=jnp.float32)
                ).astype(jnp.bfloat16)
                h_ref[slot + k + 1, :, cut] = hidden
            out = jnp.dot(wl[...], hidden, preferred_element_type=jnp.float32)
            at = r * SEGS + 8 + c * (STEP // LANES)
            for q in range(STEP // LANES):
                l_ref[at + q, 0:6, :] = out[:, q * LANES : (q + 1) * LANES]
        return carry

    lax.fori_loop(0, 11, learn_row, 0)
    for r in range(10):
        beside = l_ref[10 * SEGS + 8 + r]
        l_ref[r * SEGS] = beside
        l_ref[r * SEGS + 7] = beside

    for copy in second_a:
        copy.wait()

    def choose_row(e, carry):
        ids = aux[e * 4 + 3].astype(jnp.int32)
        low, middle, high = (ids & 1) == 1, (ids & 2) == 2, (ids & 4) == 4
        for k, (a, b) in enumerate(PAIRS):
            p = [jnp.where(low, stiff[2 * q + 1, a, b], stiff[2 * q, a, b]) for q in range(4)]
            c_ref[e * 21 + k] = jnp.where(
                high, jnp.where(middle, p[3], p[2]), jnp.where(middle, p[1], p[0])
            )
        return carry

    lax.fori_loop(7, 17, choose_row, 0)

    def stress_row(r, carry):
        e = r + 7
        stress = laminate(c_ref, e, [s_ref[e * 6 + k] for k in range(6)])
        for k in range(6):
            s_ref[e * 6 + k] = stress[k] + flat(l_ref)[pl.ds(r * (SEGS * 8) + k, SEGS, stride=8), :]
        return carry

    lax.fori_loop(0, 10, stress_row, 0)

    def residual_row(e, carry):
        force = forces_at(s_ref, e, lane)
        for f in range(3):
            v0[e * 3 + f] = (
                force[f] + aux[e * 4 + f] * dsp[e * 3 + f] - lod[(e - 8) * 3 + f]
            )
        return carry

    lax.fori_loop(8, 16, residual_row, 0)
    for side, t in ((0, 0), (1, TILES - 1)):
        for f in range(3):
            edge_c[side, f] = column(v0, 3, f, OWN, 8 + t)[...]
    moves_c = rows_to(v0, 3, 7, c_s, c_r, 0) + edges_to(edge_c, got_c, c_s, c_r, 2)
    start(moves_c)
    for t in range(TILES):
        for f in range(3):
            res_o[f, :, pl.ds(t * LANES, LANES)] = column(v0, 3, f, OWN, 8 + t)[...]
    lax.fori_loop(2, 7, choose_row, 0)
    lax.fori_loop(17, 22, choose_row, 0)
    for copy in moves_c:
        copy.wait()
    for k, (segment, row) in enumerate(landing):
        for f in range(3):
            column(v0, 3, f, row, segment)[...] = got_c[k, f]

    def mean(k):
        total = stiff[0, k, k]
        for q in range(1, 8):
            total = total + stiff[q, k, k]
        return total * 0.125

    half = 1.0 + 8.0 * jnp.maximum(mean(3), mean(4))
    center = jnp.full((1, LANES), half, jnp.float32)
    inverse = 1.0 / center

    def apply_stiffness(v, older, out, first, last):
        along_columns(lambda e: [v[e * 3 + f] for f in range(3)], y_ref, first - 2, last + 2)

        def body(e, carry):
            stress = laminate(c_ref, e, strains_at(y_ref, e))
            for k in range(6):
                s_ref[e * 6 + k] = stress[k]
            return carry

        lax.fori_loop(first - 1, last + 1, body, 0)

        def finish(e, carry):
            force = forces_at(s_ref, e, lane)
            for f in range(3):
                here = v[e * 3 + f]
                image = force[f] + aux[e * 4 + f] * here
                if older is None:
                    out[e * 3 + f] = inverse * image - here
                else:
                    out[e * 3 + f] = (2.0 * inverse) * image - 2.0 * here - older[e * 3 + f]
            return carry

        lax.fori_loop(first, last, finish, 0)

    apply_stiffness(v0, None, v1, 3, 21)
    apply_stiffness(v1, v0, v2, 5, 19)
    apply_stiffness(v2, v1, v3, 7, 17)
    along_columns(lambda e: [v3[e * 3 + f] for f in range(3)], y_ref, 7, 17)

    def folded(field):
        return field[8:16] + field[16:24]

    def sums_row(e, totals):
        strain = strains_at(y_ref, e)
        stress = laminate(c_ref, e, strain)
        energy = strain[0] * stress[0]
        for k in range(1, 6):
            energy = energy + strain[k] * stress[k]
        totals = list(totals)
        for f in range(3):
            a, b, c, d = v0[e * 3 + f], v1[e * 3 + f], v2[e * 3 + f], v3[e * 3 + f]
            energy = energy + aux[e * 4 + f] * (d * d)
            for k, product in enumerate((a * a, a * b, b * b, b * c, c * c, c * d, d * d)):
                totals[k] = totals[k] + folded(product)
        totals[7] = totals[7] + folded(energy)
        return tuple(totals)

    totals = lax.fori_loop(8, 16, sums_row, tuple(jnp.zeros((8, LANES), jnp.float32) for _ in range(8)))
    d_out[...] = jnp.concatenate([jnp.sum(t, axis=0, keepdims=True) for t in totals], axis=0)

    def shared(source, slots, sent, received, count, mine, spot, piece=None):
        copies = []
        for k in range(1, count):
            to = spot(k)
            other = lax.rem(mine + k, count)
            src = source if piece is None else source.at[other]
            copies.append(send(src, slots.at[mine], sent.at[k], received.at[mine], to))
        start(copies)
        own = source if piece is None else source.at[mine]
        slots[mine] = own[...]
        for k in range(1, count):
            other = lax.rem(mine + k, count)
            src = source if piece is None else source.at[other]
            send(src, slots.at[other], sent.at[k], received.at[other], spot(k)).wait()

    def summed(slots, count):
        total = slots[0]
        for k in range(1, count):
            total = total + slots[k]
        return total

    by_sub, by_patch = (lambda k: place(0, k)), (lambda k: place(k, 0))
    shared(d_out, d_in, d1_s, d1_r, count_s, me_s, by_sub)
    d_mid[...] = summed(d_in, count_s)
    shared(d_mid, d_in2, d2_s, d2_r, count_p, me_p, by_patch)
    everyone = jnp.sum(summed(d_in2, count_p), axis=1, keepdims=True)
    n = [jnp.broadcast_to(everyone[k : k + 1], (1, LANES)) for k in range(8)]
    n34 = (2.0 * inverse) * n[7] - 2.0 * n[6] - n[5]
    m = [n[0], n[1]]
    for k in (2, 3, 4, 5, 6):
        m.append(2.0 * n[k] - m[k % 2])
    m.append(2.0 * n34 - m[1])

    def gram(i, j):
        return 0.5 * (m[i + j] + m[abs(i - j)])

    def form(x, y):
        total, size = None, None
        for i, a in enumerate(x):
            for j, b in enumerate(y):
                term = a * b * gram(i, j)
                total = term if total is None else total + term
                size = jnp.abs(term) if size is None else size + jnp.abs(term)
        return total, size / total

    def image_of(x):
        zero = jnp.zeros((1, LANES), jnp.float32)
        out = [center * a for a in x] + [zero]
        for j, a in enumerate(x):
            if j == 0:
                out[1] = out[1] + center * a
            else:
                out[j + 1] = out[j + 1] + (0.5 * center) * a
                out[j - 1] = out[j - 1] + (0.5 * center) * a
        return out

    one = jnp.ones((1, LANES), jnp.float32)
    zero = jnp.zeros((1, LANES), jnp.float32)
    rest, way, found_y, norm = [one], [one], [zero] * 4, m[0]
    worst = one
    for step in range(ITERS):
        image = image_of(way)
        curved, spread = form(way, image)
        worst = jnp.where(spread <= TRUST, worst, 2.0 * TRUST * one)
        alpha = norm / curved
        found_y = [found_y[k] + alpha * way[k] if k < len(way) else found_y[k] for k in range(4)]
        if step + 1 < ITERS:
            rest = [(rest[k] if k < len(rest) else zero) - alpha * image[k] for k in range(len(image))]
            fresh, spread = form(rest, rest)
            worst = jnp.where(spread <= TRUST, worst, 2.0 * TRUST * one)
            beta = fresh / norm
            way = [rest[k] + (beta * way[k] if k < len(way) else zero) for k in range(len(rest))]
            norm = fresh
    trust_o[...] = jnp.broadcast_to(worst, (8, LANES))

    def adjoint_row(e, carry):
        for f in range(3):
            at = e * 3 + f
            v0[at] = found_y[0] * v0[at] + found_y[1] * v1[at] + found_y[2] * v2[at] + found_y[3] * v3[at]
        return carry

    lax.fori_loop(7, 17, adjoint_row, 0)
    for t in range(TILES):
        for f in range(3):
            adj_o[f, :, pl.ds(t * LANES, LANES)] = column(v0, 3, f, OWN, 8 + t)[...]
    along_columns(lambda e: [v0[e * 3 + f] for f in range(3)], y_ref, 7, 17)

    def upstream_row(e, carry):
        strain = strains_at(y_ref, e)
        for k in range(6):
            flat(u_ref)[pl.ds((e - 8) * (SEGS * 8) + k, SEGS, stride=8), :] = strain[k]
        return carry

    lax.fori_loop(8, 16, upstream_row, 0)

    acc_m[...] = jnp.zeros_like(acc_m)
    acc_s[...] = jnp.zeros_like(acc_s)
    wlt = wl[...].T

    def back_row(r, carry):
        slot = r * 4
        for c in range(2048 // STEP):
            cut = pl.ds(c * STEP, STEP)
            u = operand(u_ref, r, c)
            h = h_ref[slot + 3, :, cut]
            acc_s[0:6] += outer_product(u, h)
            signal = jnp.dot(wlt, u, preferred_element_type=jnp.float32)
            d = (signal * (1.0 - jnp.square(h.astype(jnp.float32)))).astype(jnp.bfloat16)
            for k in range(2, -1, -1):
                h = h_ref[slot + k, :, cut]
                acc_m[pl.ds(k * 128, 128)] += outer_product(d, h)
                signal = jnp.dot(wmt[k], d, preferred_element_type=jnp.float32)
                d = (signal * (1.0 - jnp.square(h.astype(jnp.float32)))).astype(jnp.bfloat16)
            acc_s[8:14] += outer_product(operand(x_ref, r + 1, c), d)
        return carry

    lax.fori_loop(0, 8, back_row, 0)

    whole = jnp.concatenate([acc_m[...], acc_s[...]], axis=0)
    for k in range(16):
        e_out[k, 0:25, :] = whole[25 * k : 25 * (k + 1)]
    shared(e_out, e_in, e1_s, e1_r, count_s, me_s, by_sub, piece=True)
    e_mid[...] = summed(e_in, count_s)
    shared(e_mid, e_in2, e2_s, e2_r, count_p, me_p, by_patch)
    e_end[...] = summed(e_in2, count_p)
    shared(e_end, e_in3, e3_s, e3_r, count_s, me_s, by_sub)
    whole = jnp.concatenate([e_in3[k, 0:25, :] for k in range(16)], axis=0)
    for k in range(3):
        gm_o[k] = whole[128 * k : 128 * (k + 1)]
    gl_o[...] = whole[384:390]
    gf_o[...] = whole[392:400].T[:, 0:6]


def per_device(displacement, load, foundation, layup, layup_stiffness, w_first, w_mid, w_last):
    vmem = pl.BlockSpec(memory_space=pltpu.VMEM)
    smem = pl.BlockSpec(memory_space=pltpu.SMEM)
    f32, bf16 = jnp.float32, jnp.bfloat16

    def rows(fields, count=ROWS):
        return pltpu.VMEM((count * fields, SEGS, LANES), f32)

    dma = pltpu.SemaphoreType.DMA
    out = pl.pallas_call(
        fused,
        out_shape=[
            jax.ShapeDtypeStruct(displacement.shape, f32),
            jax.ShapeDtypeStruct(displacement.shape, f32),
            jax.ShapeDtypeStruct((128, 6), f32),
            jax.ShapeDtypeStruct((3, 128, 128), f32),
            jax.ShapeDtypeStruct((6, 128), f32),
            jax.ShapeDtypeStruct((8, LANES), f32),
        ],
        in_specs=[vmem] * 4 + [smem] + [vmem] * 3,
        out_specs=[vmem] * 6,
        scratch_shapes=[
            rows(3), rows(4), rows(3, 8),
            pltpu.VMEM((2, 7, 8, LANES), f32), pltpu.VMEM((2, 3, 8, LANES), f32),
            pltpu.VMEM((6, 7, 8, LANES), f32), pltpu.VMEM((6, 3, 8, LANES), f32),
            rows(7), rows(6), rows(21),
            pltpu.VMEM((11 * SEGS, 8, LANES), f32),
            pltpu.VMEM((11 * SEGS, 8, LANES), f32),
            pltpu.VMEM((8 * SEGS, 8, LANES), f32),
            pltpu.VMEM((9 * 4, 128, 2048), bf16),
            rows(3), rows(3), rows(3), rows(3),
            pltpu.VMEM((3, 128, 128), bf16),
            pltpu.VMEM((384, 128), f32), pltpu.VMEM((16, 128), f32),
            pltpu.VMEM((8, LANES), f32), pltpu.VMEM((16, 8, LANES), f32),
            pltpu.VMEM((8, LANES), f32), pltpu.VMEM((16, 8, LANES), f32),
            pltpu.VMEM((16, 32, LANES), f32), pltpu.VMEM((16, 32, LANES), f32),
            pltpu.VMEM((32, LANES), f32), pltpu.VMEM((16, 32, LANES), f32),
            pltpu.VMEM((32, LANES), f32), pltpu.VMEM((16, 32, LANES), f32),
            dma((10,)), dma((10,)), dma((8,)), dma((8,)),
        ] + [dma((16,)) for _ in range(10)],
        compiler_params=pltpu.CompilerParams(
            collective_id=0, has_side_effects=True, vmem_limit_bytes=60 << 20
        ),
        name="adjoint_step",
    )(displacement, load, foundation, layup, layup_stiffness, w_first, w_mid, w_last)
    fast, trust = tuple(out[:5]), out[5][0, 0]
    operands = (displacement, load, foundation, layup, layup_stiffness, w_first, w_mid, w_last)
    return lax.cond(trust <= TRUST, lambda: fast, lambda: careful(*operands))


def solution(mesh):
    return jax.shard_map(
        per_device,
        mesh=mesh,
        in_specs=(
            P(None, "patch", "sub"),
            P(None, "patch", "sub"),
            P(None, "patch", "sub"),
            P("patch", "sub"),
            P(),
            P(),
            P(),
            P(),
        ),
        out_specs=(P(None, "patch", "sub"), P(None, "patch", "sub"), P(), P(), P()),
        check_vma=False,
    )
```

```python
import functools

import jax
import jax.numpy as jnp
from jax import lax
from jax.experimental import pallas as pl
from jax.experimental.pallas import tpu as pltpu
from jax.sharding import PartitionSpec as P

ITERS = 4
PATCH_SUB = ("patch", "sub")
PATCH = "patch"
SUB = "sub"


BASIS_VALUE = (0.125, 0.75, 0.125)
BASIS_SLOPE = (-0.5, 0.0, 0.5)
BASIS_CURVE = (1.0, -2.0, 1.0)
HOOP_CURVATURE = 0.25


def by_axis(value, axes):
    return lax.psum(value, axes)


def padded_2(cells, sides, width):
    for axis, dim in sides:
        count = lax.axis_size(axis)
        head = lax.slice_in_dim(cells, 0, width, axis=dim)
        tail = lax.slice_in_dim(cells, cells.shape[dim] - width, cells.shape[dim], axis=dim)
        cells = jnp.concatenate(
            [
                lax.ppermute(tail, axis, [(i, (i + 1) % count) for i in range(count)]),
                cells,
                lax.ppermute(head, axis, [((i + 1) % count, i) for i in range(count)]),
            ],
            axis=dim,
        )
    return cells


def split_up(value, dim, size):
    lengths = value.shape
    pieces = value.reshape(*lengths[:dim], size, lengths[dim] // size, *lengths[dim + 1 :])
    return jnp.moveaxis(pieces, dim, 0)


def sent_and_summed(value, axis, dim):
    size = lax.axis_size(axis)
    pieces = lax.all_to_all(split_up(value, dim, size), axis, 0, 0, tiled=True)
    return jnp.sum(pieces, axis=0)


def sent_to_all(value, axis):
    size = lax.axis_size(axis)
    return lax.all_to_all(
        jnp.broadcast_to(value[None], (size, *value.shape)), axis, 0, 0, tiled=True
    )


def of_everyone(value, axis):
    return sent_to_all(value, axis).sum(axis=0)


def packed_total(arrays, axis):
    vector, at, done = (jnp.concatenate([a.reshape(-1) for a in arrays]), 0, [])
    subtotal = of_everyone(vector, axis)
    for a in arrays:
        done.append(subtotal[at : at + a.size].reshape(a.shape))
        at += a.size
    return tuple(done)


def turned_gather(arrays, axis, dims):
    turned = [jnp.moveaxis(a, dim, 0) for a, dim in zip(arrays, dims)]
    both = jnp.concatenate([t.reshape(len(t), -1) for t in turned], axis=1)
    filled, at, done = (lax.all_gather(both, axis, axis=0, tiled=True), 0, [])
    for t, dim in zip(turned, dims):
        section = filled[:, at : at + t[0].size].reshape(-1, *t.shape[1:])
        done.append(jnp.moveaxis(section, 0, dim))
        at += t[0].size
    return tuple(done)


def correlate(padded, along_x, along_y):
    row_count = padded.shape[-2] - 2
    col_count = padded.shape[-1] - 2
    partial_x = None
    for offset in range(3):
        if along_x[offset] != 0.0:
            weighted = along_x[offset] * padded[..., offset : offset + row_count, :]
            partial_x = weighted if partial_x is None else partial_x + weighted
    running = None
    for offset in range(3):
        if along_y[offset] != 0.0:
            weighted = along_y[offset] * partial_x[..., offset : offset + col_count]
            running = weighted if running is None else running + weighted
    return running


def mirrored(padded, along_x, along_y):
    return correlate(padded, along_x[::-1], along_y[::-1])


def strains(padded):
    along_u, along_v, along_w = (padded[0], padded[1], padded[2])
    return jnp.stack(
        [
            correlate(along_u, BASIS_SLOPE, BASIS_VALUE),
            correlate(along_v, BASIS_VALUE, BASIS_SLOPE)
            + HOOP_CURVATURE * correlate(along_w, BASIS_VALUE, BASIS_VALUE),
            correlate(along_u, BASIS_VALUE, BASIS_SLOPE)
            + correlate(along_v, BASIS_SLOPE, BASIS_VALUE),
            -correlate(along_w, BASIS_CURVE, BASIS_VALUE),
            -correlate(along_w, BASIS_VALUE, BASIS_CURVE),
            -2.0 * correlate(along_w, BASIS_SLOPE, BASIS_SLOPE),
        ]
    )


def forces(spread):
    force_u = mirrored(spread[0], BASIS_SLOPE, BASIS_VALUE) + mirrored(
        spread[2], BASIS_VALUE, BASIS_SLOPE
    )
    force_v = mirrored(spread[1], BASIS_VALUE, BASIS_SLOPE) + mirrored(
        spread[2], BASIS_SLOPE, BASIS_VALUE
    )
    force_w = (
        HOOP_CURVATURE * mirrored(spread[1], BASIS_VALUE, BASIS_VALUE)
        - mirrored(spread[3], BASIS_CURVE, BASIS_VALUE)
        - mirrored(spread[4], BASIS_VALUE, BASIS_CURVE)
        - 2.0 * mirrored(spread[5], BASIS_SLOPE, BASIS_SLOPE)
    )
    return jnp.stack([force_u, force_v, force_w])


def apply_layup(stiffness_map, strain):
    running = stiffness_map[:, 0] * strain[0]
    for column in range(1, 6):
        running = running + stiffness_map[:, column] * strain[column]
    return running


def outer_product(left, right):
    return lax.dot_general(
        left, right, (((1,), (1,)), ((), ())), preferred_element_type=jnp.float32
    )


def forward_mlp(inputs, w_first, w_mid, w_last):
    hidden_layer = jnp.tanh(jnp.dot(w_first, inputs, preferred_element_type=jnp.float32)).astype(
        jnp.bfloat16
    )
    activations = [hidden_layer]
    for layer_index in range(w_mid.shape[0]):
        hidden_layer = jnp.tanh(
            jnp.dot(w_mid[layer_index], hidden_layer, preferred_element_type=jnp.float32)
        ).astype(jnp.bfloat16)
        activations.append(hidden_layer)
    return (jnp.dot(w_last, hidden_layer, preferred_element_type=jnp.float32), activations)


def backward_mlp(inputs, activations, upstream, w_mid, w_last):
    grad_last = outer_product(upstream, activations[-1])
    signal = jnp.dot(w_last.T, upstream, preferred_element_type=jnp.float32)
    derivative = (signal * (1.0 - jnp.square(activations[-1].astype(jnp.float32)))).astype(
        jnp.bfloat16
    )
    mid_grads = []
    for layer_index in range(w_mid.shape[0] - 1, -1, -1):
        mid_grads.append(outer_product(derivative, activations[layer_index]))
        signal = jnp.dot(w_mid[layer_index].T, derivative, preferred_element_type=jnp.float32)
        derivative = (
            signal * (1.0 - jnp.square(activations[layer_index].astype(jnp.float32)))
        ).astype(jnp.bfloat16)
    grad_first = outer_product(derivative, inputs)
    return (grad_first, jnp.stack(mid_grads[::-1]), grad_last)


def two_products(remainder, mapped):
    return (
        by_axis(jnp.sum(remainder * remainder), PATCH_SUB),
        by_axis(jnp.sum(remainder * mapped), PATCH_SUB),
    )


def careful(displacement, load, foundation, layup, layup_stiffness, w_first, w_mid, w_last):
    layup_count = layup_stiffness.shape[0]

    def coefficients(layup_ids):
        onehot = (
            layup_ids[None] == jnp.arange(layup_count, dtype=jnp.int32)[:, None, None]
        ).astype(jnp.float32)
        return jnp.einsum("lab,lxy->abxy", layup_stiffness, onehot, precision=lax.Precision.HIGHEST)

    stiffness_map = coefficients(layup)
    wide_ids = padded_2(layup, ((PATCH, 0), (SUB, 1)), 1)
    stiffness_wide = coefficients(wide_ids)

    def operate(search):
        padded = padded_2(search, ((PATCH, 1), (SUB, 2)), 2)
        return forces(apply_layup(stiffness_wide, strains(padded))) + foundation * search

    padded = padded_2(displacement, ((PATCH, 1), (SUB, 2)), 1)
    strain = strains(padded)
    inputs = strain.reshape(6, -1).astype(jnp.bfloat16)
    learned, activations = forward_mlp(inputs, w_first, w_mid, w_last)
    stress = apply_layup(stiffness_map, strain) + learned.reshape(strain.shape)
    spread = padded_2(stress, ((PATCH, 1), (SUB, 2)), 1)
    residual = forces(spread) + foundation * displacement - load
    adjoint = jnp.zeros_like(residual)
    remainder = residual
    mapped = operate(remainder)
    norm_now, curved = two_products(remainder, mapped)
    step_size = norm_now / curved
    direction, mapped_dir = (remainder, mapped)
    for step_index in range(ITERS):
        adjoint = adjoint + step_size * direction
        remainder = remainder - step_size * mapped_dir
        if step_index + 1 < ITERS:
            mapped = operate(remainder)
            norm_next, curved = two_products(remainder, mapped)
            beta_ratio = norm_next / norm_now
            step_size = norm_next / (curved - beta_ratio * norm_next / step_size)
            direction = remainder + beta_ratio * direction
            mapped_dir = mapped + beta_ratio * mapped_dir
            norm_now = norm_next
    cycle = padded_2(adjoint, ((PATCH, 1), (SUB, 2)), 1)
    upstream = strains(cycle).reshape(6, -1).astype(jnp.bfloat16)
    grad_first, grad_mid, grad_last = backward_mlp(inputs, activations, upstream, w_mid, w_last)
    shares = (
        sent_and_summed(grad_first, SUB, 0),
        sent_and_summed(grad_mid, SUB, 1),
        sent_and_summed(grad_last, SUB, 1),
    )
    crossed = packed_total((shares[0], shares[1], shares[2]), PATCH)
    totals = turned_gather((crossed[0], crossed[1], crossed[2]), SUB, (0, 1, 1))
    return (residual, adjoint, totals[0], totals[1], totals[2])


ROWS = 24
SEGS = 24
LANES = 128
OWN = 8
TILES = 16
STEP = 512
TRUST = 400.0
MESH = pl.DeviceIdType.MESH
PAIRS = [(a, b) for a in range(6) for b in range(a, 6)]
SPOT = {pair: k for k, pair in enumerate(PAIRS)}


def flat(ref):
    lead, mid, lanes = ref.shape
    return ref.reshape(lead * mid, lanes)


def column(ref, fields, field, row, segment):
    return flat(ref).at[pl.ds((row * fields + field) * SEGS + segment, 8, stride=fields * SEGS), :]


def lane_of():
    return lax.broadcasted_iota(jnp.int32, (SEGS, LANES), 1)


def after(field, lane):
    turned = pltpu.roll(field, LANES - 1, 1)
    return jnp.where(lane == LANES - 1, pltpu.roll(turned, SEGS - 1, 0), turned)


def before(field, lane):
    turned = pltpu.roll(field, 1, 1)
    return jnp.where(lane == 0, pltpu.roll(turned, 1, 0), turned)


def along_columns(read, y_ref, first, last):
    lane = lane_of()

    def body(e, carry):
        u, v, w = read(e)
        at = e * 7
        for k, field in enumerate((u, v, w)):
            ahead, behind = after(field, lane), before(field, lane)
            both = ahead + behind
            y_ref[at + 2 * k] = 0.75 * field + 0.125 * both
            y_ref[at + 2 * k + 1] = 0.5 * (ahead - behind)
            if k == 2:
                y_ref[at + 6] = both - 2.0 * field
        return carry

    lax.fori_loop(first, last, body, 0, unroll=2)


def strains_at(y_ref, e):
    at = e * 7

    def three(k):
        return y_ref[at - 7 + k], y_ref[at + k], y_ref[at + 7 + k]

    def value(k):
        m, c, p = three(k)
        return 0.75 * c + 0.125 * (p + m)

    def slope(k):
        return 0.5 * (y_ref[at + 7 + k] - y_ref[at - 7 + k])

    m, c, p = three(4)
    pair = p + m
    return [
        slope(0),
        value(3) + HOOP_CURVATURE * (0.75 * c + 0.125 * pair),
        value(1) + slope(2),
        2.0 * c - pair,
        -value(6),
        y_ref[at - 7 + 5] - y_ref[at + 7 + 5],
    ]


def laminate(c_ref, e, strain):
    at = e * 21
    total = [None] * 6
    for (a, b), k in SPOT.items():
        c = c_ref[at + k]
        term = c * strain[b]
        total[a] = term if total[a] is None else total[a] + term
        if a != b:
            term = c * strain[a]
            total[b] = term if total[b] is None else total[b] + term
    return total


def forces_at(s_ref, e, lane):
    at = e * 6

    def three(k):
        return s_ref[at - 6 + k], s_ref[at + k], s_ref[at + 6 + k]

    def value(k):
        m, c, p = three(k)
        return 0.75 * c + 0.125 * (p + m)

    def slope(k):
        return 0.5 * (s_ref[at - 6 + k] - s_ref[at + 6 + k])

    def spread(here, behind, ahead):
        return here + before(behind, lane) + after(ahead, lane)

    a, b = slope(0), value(2)
    force_u = spread(0.75 * a, 0.125 * a + 0.5 * b, 0.125 * a - 0.5 * b)
    a, b = slope(2), value(1)
    force_v = spread(0.75 * a, 0.125 * a + 0.5 * b, 0.125 * a - 0.5 * b)
    m, c, p = three(3)
    a = HOOP_CURVATURE * b - ((m + p) - 2.0 * c)
    d = value(4)
    half = slope(5)
    base = 0.125 * a - d
    force_w = spread(0.75 * a + 2.0 * d, base - half, base + half)
    return force_u, force_v, force_w


def fused(
    disp, load, found, lay, stiff, w1t, wm, wl,
    res_o, adj_o, gf_o, gm_o, gl_o, trust_o,
    dsp, aux, ids, lod, edge_a, edge_c, got_a, got_c, y_ref, s_ref, c_ref, x_ref, l_ref, u_ref, h_ref,
    v0, v1, v2, v3, wmt, acc_m, acc_s,
    d_out, d_in, d_mid, d_in2, e_out, e_in, e_mid, e_in2, e_end, e_in3,
    g_out, g_in, g_mid, g_in2, g_end, g_in3,
    a_s, a_r, c_s, c_r, d1_s, d1_r, d2_s, d2_r, e1_s, e1_r, e2_s, e2_r, e3_s, e3_r,
    g1_s, g1_r, g2_s, g2_r, g3_s, g3_r,
):
    me_p, me_s = lax.axis_index("patch"), lax.axis_index("sub")
    count_p, count_s = lax.axis_size("patch"), lax.axis_size("sub")

    def place(dp, ds):
        return {"patch": lax.rem(me_p + dp, count_p), "sub": lax.rem(me_s + ds, count_s)}

    up, down = count_p - 1, 1
    left, right = count_s - 1, 1
    greeted = [(0, k) for k in range(1, count_s)] + [(k, 0) for k in range(1, count_p)]
    greeted += [(a, b) for a in (up, down) for b in (left, right)]
    barrier = pltpu.get_barrier_semaphore()
    for dp, ds in greeted:
        pl.semaphore_signal(barrier, inc=1, device_id=place(dp, ds), device_id_type=MESH)

    for t in range(TILES):
        cut = pl.ds(t * LANES, LANES)
        for f in range(3):
            column(dsp, 3, f, OWN, 8 + t)[...] = disp[f, :, cut]
        column(ids, 1, 0, OWN, 8 + t)[...] = lay[:, cut].astype(jnp.float32)
    ends = ((0, pl.ds(0, LANES)), (1, pl.ds((TILES - 1) * LANES, LANES)))
    for side, cut in ends:
        for f in range(3):
            edge_a[side, f] = disp[f, :, cut]
            edge_a[side, 3 + f] = found[f, :, cut]
        edge_a[side, 6] = lay[:, cut].astype(jnp.float32)

    pl.semaphore_wait(barrier, len(greeted))

    def send(src, dst, sent, received, to):
        return pltpu.make_async_remote_copy(
            src_ref=src, dst_ref=dst, send_sem=sent, recv_sem=received, device_id=to, device_id_type=MESH
        )

    def rows_to(ref, fields, near, far, sent, received, first):
        own, n = pl.ds(OWN, TILES), (far - near) * fields
        below = send(
            ref.at[pl.ds((16 - far) * fields, n), own, :],
            ref.at[pl.ds((8 - far) * fields, n), own, :],
            sent.at[first], received.at[first], place(down, 0),
        )
        above = send(
            ref.at[pl.ds((8 + near) * fields, n), own, :],
            ref.at[pl.ds((16 + near) * fields, n), own, :],
            sent.at[first + 1], received.at[first + 1], place(up, 0),
        )
        return [below, above]

    heading = ((0, right, 1), (0, left, 0), (down, right, 1), (down, left, 0), (up, right, 1), (up, left, 0))

    def edges_to(edge, got, sent, received, first):
        return [
            send(edge.at[side], got.at[k], sent.at[first + k], received.at[first + k], place(dp, ds))
            for k, (dp, ds, side) in enumerate(heading)
        ]

    def start(copies):
        for copy in copies:
            copy.start()

    landing = ((7, 8), (0, 8), (7, 0), (0, 0), (7, 16), (0, 16))

    first_a = (
        rows_to(dsp, 3, 0, 2, a_s, a_r, 0)
        + edges_to(edge_a, got_a, a_s, a_r, 2)
        + rows_to(ids, 1, 0, 1, a_s, a_r, 8)
    )
    start(first_a)
    for t in range(TILES):
        cut = pl.ds(t * LANES, LANES)
        for f in range(3):
            column(aux, 3, f, OWN, 8 + t)[...] = found[f, :, cut]
            column(lod, 3, f, 0, 8 + t)[...] = load[f, :, cut]
    for k in range(3):
        wmt[k] = wm[k].T
    w1 = w1t[...].T
    wlt = wl[...].T

    def choose_row(e, carry):
        kind = ids[e].astype(jnp.int32)
        low, middle, high = (kind & 1) == 1, (kind & 2) == 2, (kind & 4) == 4
        for k, (a, b) in enumerate(PAIRS):
            p = [jnp.where(low, stiff[a, 2 * q + 1, b], stiff[a, 2 * q, b]) for q in range(4)]
            c_ref[e * 21 + k] = jnp.where(
                high, jnp.where(middle, p[3], p[2]), jnp.where(middle, p[1], p[0])
            )
        return carry

    for copy in first_a:
        copy.wait()
    for k, (segment, row) in enumerate(landing):
        for f in range(3):
            column(dsp, 3, f, row, segment)[...] = got_a[k, f]
            column(aux, 3, f, row, segment)[...] = got_a[k, 3 + f]
        column(ids, 1, 0, row, segment)[...] = got_a[k, 6]
    second_a = rows_to(aux, 3, 0, 5, a_s, a_r, 10) + rows_to(ids, 1, 1, 6, a_s, a_r, 12)
    start(second_a)
    lax.fori_loop(7, 17, choose_row, 0)

    lane = lane_of()
    along_columns(lambda e: [dsp[e * 3 + f] for f in range(3)], y_ref, 6, 18)

    def strain_row(r, carry):
        e = r + 7
        strain = strains_at(y_ref, e)
        for k in range(6):
            s_ref[e * 6 + k] = strain[k]
            flat(x_ref)[pl.ds(r * (SEGS * 8) + k, SEGS, stride=8), :] = strain[k]
        return carry

    lax.fori_loop(0, 10, strain_row, 0)
    tile_lane = lax.broadcasted_iota(jnp.int32, (8, LANES), 1)
    beside = 10 * SEGS
    packed = jnp.zeros((8, LANES), jnp.float32)
    for r in range(10):
        ends_of = jnp.where(tile_lane < 64, x_ref[r * SEGS], x_ref[r * SEGS + 7])
        turned = pltpu.roll(ends_of, 2 * r + 1, 1)
        packed = jnp.where((tile_lane == 2 * r) | (tile_lane == 2 * r + 1), turned, packed)
    x_ref[beside] = packed

    def operand(ref, at, width):
        tiles = [ref[at + q] for q in range(width // LANES)]
        return jnp.concatenate(tiles, axis=1)[:6].astype(jnp.bfloat16)

    def learn(parts):
        for at, slot, first, width in parts:
            h_ref[slot, :, pl.ds(first, width)] = jnp.tanh(
                jnp.dot(w1, operand(x_ref, at, width), preferred_element_type=jnp.float32)
            ).astype(jnp.bfloat16)
        for k in range(3):
            for at, slot, first, width in parts:
                cut = pl.ds(first, width)
                h_ref[slot + k + 1, :, cut] = jnp.tanh(
                    jnp.dot(wm[k], h_ref[slot + k, :, cut], preferred_element_type=jnp.float32)
                ).astype(jnp.bfloat16)
        for at, slot, first, width in parts:
            out = jnp.dot(wl[...], h_ref[slot + 3, :, pl.ds(first, width)], preferred_element_type=jnp.float32)
            for q in range(width // LANES):
                l_ref[at + q, 0:6, :] = out[:, q * LANES : (q + 1) * LANES]

    def row_parts(r, slot):
        return [
            (r * SEGS + 8 + c * (STEP // LANES), slot, c * STEP, STEP) for c in range(2048 // STEP)
        ]

    def stress_row(r, carry):
        e = r + 7
        stress = laminate(c_ref, e, [s_ref[e * 6 + k] for k in range(6)])
        for k in range(6):
            s_ref[e * 6 + k] = stress[k] + flat(l_ref)[pl.ds(r * (SEGS * 8) + k, SEGS, stride=8), :]
        return carry

    learn([(beside, 32, 0, LANES)] + row_parts(0, 36))
    for r in range(10):
        turned = pltpu.roll(l_ref[beside], LANES - 1 - 2 * r, 1)
        l_ref[r * SEGS] = turned
        l_ref[r * SEGS + 7] = turned
    learn(row_parts(1, 0))
    stress_row(0, 0)
    stress_row(1, 0)

    def rows_of_group(g):
        own, at = pl.ds(OWN, TILES), g * 6
        return [
            send(v0.at[pl.ds(24 + at, 6), own, :], v0.at[pl.ds(at, 6), own, :],
                 c_s.at[6 + g], c_r.at[6 + g], place(down, 0)),
            send(v0.at[pl.ds(24 + at, 6), own, :], v0.at[pl.ds(48 + at, 6), own, :],
                 c_s.at[10 + g], c_r.at[10 + g], place(up, 0)),
        ]

    def group(g, carry):
        r = 2 * g + 2
        learn(row_parts(r, (r - 1) * 4) + row_parts(r + 1, jnp.where(g == 3, 32, r * 4)))
        for k in range(2):
            stress_row(r + k, 0)
        for k in range(2):
            e = 8 + 2 * g + k
            force = forces_at(s_ref, e, lane)
            for f in range(3):
                v0[e * 3 + f] = force[f] + aux[e * 3 + f] * dsp[e * 3 + f] - lod[(e - 8) * 3 + f]
        start(rows_of_group(g))
        return carry

    lax.fori_loop(0, 4, group, 0)
    for side, t in ((0, 0), (1, TILES - 1)):
        for f in range(3):
            edge_c[side, f] = column(v0, 3, f, OWN, 8 + t)[...]
    moves_c = edges_to(edge_c, got_c, c_s, c_r, 0)
    start(moves_c)
    for copy in second_a:
        copy.wait()
    lax.fori_loop(2, 7, choose_row, 0)
    lax.fori_loop(17, 22, choose_row, 0)
    for t in range(TILES):
        for f in range(3):
            res_o[f, :, pl.ds(t * LANES, LANES)] = column(v0, 3, f, OWN, 8 + t)[...]
    for copy in moves_c:
        copy.wait()
    for g in range(4):
        for copy in rows_of_group(g):
            copy.wait()
    for k, (segment, row) in enumerate(landing):
        for f in range(3):
            column(v0, 3, f, row, segment)[...] = got_c[k, f]

    def mean(k):
        total = stiff[k, 0, k]
        for q in range(1, 8):
            total = total + stiff[k, q, k]
        return total * 0.125

    half = 1.0 + 8.0 * jnp.maximum(mean(3), mean(4))
    center = jnp.full((1, LANES), half, jnp.float32)
    inverse = 1.0 / center

    def apply_stiffness(v, older, out, first, last):
        along_columns(lambda e: [v[e * 3 + f] for f in range(3)], y_ref, first - 2, last + 2)

        def body(e, carry):
            stress = laminate(c_ref, e, strains_at(y_ref, e))
            for k in range(6):
                s_ref[e * 6 + k] = stress[k]
            return carry

        lax.fori_loop(first - 1, last + 1, body, 0)

        def finish(e, carry):
            force = forces_at(s_ref, e, lane)
            for f in range(3):
                here = v[e * 3 + f]
                image = force[f] + aux[e * 3 + f] * here
                if older is None:
                    out[e * 3 + f] = inverse * image - here
                else:
                    out[e * 3 + f] = (2.0 * inverse) * image - 2.0 * here - older[e * 3 + f]
            return carry

        lax.fori_loop(first, last, finish, 0)

    apply_stiffness(v0, None, v1, 3, 21)
    apply_stiffness(v1, v0, v2, 5, 19)
    apply_stiffness(v2, v1, v3, 7, 17)
    along_columns(lambda e: [v3[e * 3 + f] for f in range(3)], y_ref, 7, 17)

    def folded(field):
        return field[8:16] + field[16:24]

    def sums_row(e, totals):
        strain = strains_at(y_ref, e)
        stress = laminate(c_ref, e, strain)
        energy = strain[0] * stress[0]
        for k in range(1, 6):
            energy = energy + strain[k] * stress[k]
        totals = list(totals)
        for f in range(3):
            a, b, c, d = v0[e * 3 + f], v1[e * 3 + f], v2[e * 3 + f], v3[e * 3 + f]
            energy = energy + aux[e * 3 + f] * (d * d)
            for k, product in enumerate((a * a, a * b, b * b, b * c, c * c, c * d, d * d)):
                totals[k] = totals[k] + folded(product)
        totals[7] = totals[7] + folded(energy)
        return tuple(totals)

    totals = lax.fori_loop(8, 16, sums_row, tuple(jnp.zeros((8, LANES), jnp.float32) for _ in range(8)))
    d_out[...] = jnp.concatenate([jnp.sum(t, axis=0, keepdims=True) for t in totals], axis=0)

    def shared(source, slots, sent, received, count, mine, spot, piece=None):
        copies = []
        for k in range(1, count):
            src = source if piece is None else source.at[lax.rem(mine + k, count)]
            copies.append(send(src, slots.at[mine], sent.at[k], received.at[mine], spot(k)))
        start(copies)
        own = source if piece is None else source.at[mine]
        slots[mine] = own[...]

        def finish():
            for k in range(1, count):
                other = lax.rem(mine + k, count)
                src = source if piece is None else source.at[other]
                send(src, slots.at[other], sent.at[k], received.at[other], spot(k)).wait()

        return finish

    def summed(slots, count):
        total = slots[0]
        for k in range(1, count):
            total = total + slots[k]
        return total

    by_sub, by_patch = (lambda k: place(0, k)), (lambda k: place(k, 0))
    shared(d_out, d_in, d1_s, d1_r, count_s, me_s, by_sub)()
    d_mid[...] = summed(d_in, count_s)
    shared(d_mid, d_in2, d2_s, d2_r, count_p, me_p, by_patch)()
    everyone = jnp.sum(summed(d_in2, count_p), axis=1, keepdims=True)
    n = [jnp.broadcast_to(everyone[k : k + 1], (1, LANES)) for k in range(8)]
    n34 = (2.0 * inverse) * n[7] - 2.0 * n[6] - n[5]
    m = [n[0], n[1]]
    for k in (2, 3, 4, 5, 6):
        m.append(2.0 * n[k] - m[k % 2])
    m.append(2.0 * n34 - m[1])

    def gram(i, j):
        return 0.5 * (m[i + j] + m[abs(i - j)])

    def form(x, y):
        total, size = None, None
        for i, a in enumerate(x):
            for j, b in enumerate(y):
                term = a * b * gram(i, j)
                total = term if total is None else total + term
                size = jnp.abs(term) if size is None else size + jnp.abs(term)
        return total, size / total

    def image_of(x):
        zero = jnp.zeros((1, LANES), jnp.float32)
        out = [center * a for a in x] + [zero]
        for j, a in enumerate(x):
            if j == 0:
                out[1] = out[1] + center * a
            else:
                out[j + 1] = out[j + 1] + (0.5 * center) * a
                out[j - 1] = out[j - 1] + (0.5 * center) * a
        return out

    one = jnp.ones((1, LANES), jnp.float32)
    zero = jnp.zeros((1, LANES), jnp.float32)
    rest, way, found_y, norm = [one], [one], [zero] * 4, m[0]
    worst = one
    for step in range(ITERS):
        image = image_of(way)
        curved, spread = form(way, image)
        worst = jnp.where(spread <= TRUST, worst, 2.0 * TRUST * one)
        alpha = norm / curved
        found_y = [found_y[k] + alpha * way[k] if k < len(way) else found_y[k] for k in range(4)]
        if step + 1 < ITERS:
            rest = [(rest[k] if k < len(rest) else zero) - alpha * image[k] for k in range(len(image))]
            fresh, spread = form(rest, rest)
            worst = jnp.where(spread <= TRUST, worst, 2.0 * TRUST * one)
            beta = fresh / norm
            way = [rest[k] + (beta * way[k] if k < len(way) else zero) for k in range(len(rest))]
            norm = fresh
    trust_o[0, 0] = worst[0, 0]

    def adjoint_row(e, carry):
        for f in range(3):
            at = e * 3 + f
            v0[at] = found_y[0] * v0[at] + found_y[1] * v1[at] + found_y[2] * v2[at] + found_y[3] * v3[at]
        return carry

    lax.fori_loop(7, 17, adjoint_row, 0)
    for t in range(TILES):
        for f in range(3):
            adj_o[f, :, pl.ds(t * LANES, LANES)] = column(v0, 3, f, OWN, 8 + t)[...]
    along_columns(lambda e: [v0[e * 3 + f] for f in range(3)], y_ref, 7, 17)

    def upstream_row(e, carry):
        strain = strains_at(y_ref, e)
        for k in range(6):
            flat(u_ref)[pl.ds((e - 8) * (SEGS * 8) + k, SEGS, stride=8), :] = strain[k]
        return carry

    lax.fori_loop(8, 16, upstream_row, 0)

    acc_m[...] = jnp.zeros_like(acc_m)
    acc_s[...] = jnp.zeros_like(acc_s)

    def derive(weights, signal_of, slot):
        for c in range(2048 // STEP):
            cut = pl.ds(c * STEP, STEP)
            h = h_ref[slot, :, cut].astype(jnp.float32)
            signal = jnp.dot(weights, signal_of(c, cut), preferred_element_type=jnp.float32)
            h_ref[slot, :, cut] = (signal * (1.0 - jnp.square(h))).astype(jnp.bfloat16)

    def back_last(r, carry):
        slot = r * 4 + 3
        u = operand(u_ref, r * SEGS + 8, 2048)
        acc_s[0:6] += outer_product(u, h_ref[slot])
        derive(wlt, lambda c, cut: u[:, c * STEP : (c + 1) * STEP], slot)
        return carry

    def back_mid(k):
        def body(r, carry):
            slot = r * 4 + k
            acc_m[k] += outer_product(h_ref[slot + 1], h_ref[slot])
            derive(wmt[k], lambda c, cut: h_ref[slot + 1, :, cut], slot)
            return carry

        lax.fori_loop(0, 8, body, 0)

    def back_first(r, carry):
        acc_s[8:14] += outer_product(operand(x_ref, (r + 1) * SEGS + 8, 2048), h_ref[r * 4])
        return carry

    lax.fori_loop(0, 8, back_last, 0)
    back_mid(2)
    back_mid(1)
    for k in range(16):
        e_out[k, 0:8, :] = acc_m[1, 8 * k : 8 * k + 8]
        e_out[k, 8:16, :] = acc_m[2, 8 * k : 8 * k + 8]
    finish_e1 = shared(e_out, e_in, e1_s, e1_r, count_s, me_s, by_sub, piece=True)
    back_mid(0)
    finish_e1()
    e_mid[...] = summed(e_in, count_s)
    finish_e2 = shared(e_mid, e_in2, e2_s, e2_r, count_p, me_p, by_patch)
    lax.fori_loop(0, 8, back_first, 0)
    for k in range(16):
        g_out[k, 0:8, :] = acc_m[0, 8 * k : 8 * k + 8]
        g_out[k, 8:9, :] = acc_s[k : k + 1]
    finish_g1 = shared(g_out, g_in, g1_s, g1_r, count_s, me_s, by_sub, piece=True)
    finish_g1()
    g_mid[...] = summed(g_in, count_s)
    finish_g2 = shared(g_mid, g_in2, g2_s, g2_r, count_p, me_p, by_patch)
    finish_e2()
    e_end[...] = summed(e_in2, count_p)
    finish_e3 = shared(e_end, e_in3, e3_s, e3_r, count_s, me_s, by_sub)
    finish_g2()
    g_end[...] = summed(g_in2, count_p)
    finish_g3 = shared(g_end, g_in3, g3_s, g3_r, count_s, me_s, by_sub)
    finish_e3()
    for k in range(16):
        gm_o[1, 8 * k : 8 * k + 8] = e_in3[k, 0:8, :]
        gm_o[2, 8 * k : 8 * k + 8] = e_in3[k, 8:16, :]
    finish_g3()
    for k in range(16):
        gm_o[0, 8 * k : 8 * k + 8] = g_in3[k, 0:8, :]
    for k in range(6):
        gl_o[k : k + 1] = g_in3[k, 8:9, :]
        gf_o[k : k + 1] = g_in3[8 + k, 8:9, :]


def per_device(displacement, load, foundation, layup, layup_stiffness, w_first, w_mid, w_last):
    vmem = pl.BlockSpec(memory_space=pltpu.VMEM)
    smem = pl.BlockSpec(memory_space=pltpu.SMEM)
    f32, bf16 = jnp.float32, jnp.bfloat16

    def rows(fields, count=ROWS):
        return pltpu.VMEM((count * fields, SEGS, LANES), f32)

    dma = pltpu.SemaphoreType.DMA
    out = pl.pallas_call(
        fused,
        out_shape=[
            jax.ShapeDtypeStruct(displacement.shape, f32),
            jax.ShapeDtypeStruct(displacement.shape, f32),
            jax.ShapeDtypeStruct((6, 128), f32),
            jax.ShapeDtypeStruct((3, 128, 128), f32),
            jax.ShapeDtypeStruct((6, 128), f32),
            jax.ShapeDtypeStruct((1, 1), f32),
        ],
        in_specs=[vmem] * 4 + [smem] + [vmem] * 3,
        out_specs=[vmem] * 5 + [smem],
        scratch_shapes=[
            rows(3), rows(3), rows(1), rows(3, 8),
            pltpu.VMEM((2, 7, 8, LANES), f32), pltpu.VMEM((2, 3, 8, LANES), f32),
            pltpu.VMEM((6, 7, 8, LANES), f32), pltpu.VMEM((6, 3, 8, LANES), f32),
            rows(7), rows(6), rows(21),
            pltpu.VMEM((11 * SEGS, 8, LANES), f32),
            pltpu.VMEM((11 * SEGS, 8, LANES), f32),
            pltpu.VMEM((8 * SEGS, 8, LANES), f32),
            pltpu.VMEM((10 * 4, 128, 2048), bf16),
            rows(3), rows(3), rows(3), rows(3),
            pltpu.VMEM((3, 128, 128), bf16),
            pltpu.VMEM((3, 128, 128), f32), pltpu.VMEM((16, 128), f32),
            pltpu.VMEM((8, LANES), f32), pltpu.VMEM((16, 8, LANES), f32),
            pltpu.VMEM((8, LANES), f32), pltpu.VMEM((16, 8, LANES), f32),
        ] + [
            pltpu.VMEM(shape, f32)
            for n in (16, 9)
            for shape in [(16, n, LANES), (16, n, LANES), (n, LANES)] + [(16, n, LANES), (n, LANES), (16, n, LANES)]
        ] + [
            dma((14,)), dma((14,)), dma((14,)), dma((14,)),
        ] + [dma((16,)) for _ in range(16)],
        compiler_params=pltpu.CompilerParams(
            collective_id=0, has_side_effects=True, vmem_limit_bytes=52 << 20
        ),
        name="adjoint_step",
    )(
        displacement, load, foundation, layup, layup_stiffness.transpose(1, 0, 2), w_first.T, w_mid, w_last
    )
    fast, trust = (out[0], out[1], out[2].T, out[3], out[4]), out[5][0, 0]
    operands = (displacement, load, foundation, layup, layup_stiffness, w_first, w_mid, w_last)
    return lax.cond(trust <= TRUST, lambda: fast, lambda: careful(*operands))


def solution(mesh):
    return jax.shard_map(
        per_device,
        mesh=mesh,
        in_specs=(
            P(None, "patch", "sub"),
            P(None, "patch", "sub"),
            P(None, "patch", "sub"),
            P("patch", "sub"),
            P(),
            P(),
            P(),
            P(),
        ),
        out_specs=(P(None, "patch", "sub"), P(None, "patch", "sub"), P(), P(), P()),
        check_vma=False,
    )
```

```python
import functools

import jax
import jax.numpy as jnp
from jax import lax
from jax.experimental import pallas as pl
from jax.experimental.pallas import tpu as pltpu
from jax.sharding import PartitionSpec as P

ITERS = 4
PATCH_SUB = ("patch", "sub")
PATCH = "patch"
SUB = "sub"


BASIS_VALUE = (0.125, 0.75, 0.125)
BASIS_SLOPE = (-0.5, 0.0, 0.5)
BASIS_CURVE = (1.0, -2.0, 1.0)
HOOP_CURVATURE = 0.25


def by_axis(value, axes):
    return lax.psum(value, axes)


def padded_2(cells, sides, width):
    for axis, dim in sides:
        count = lax.axis_size(axis)
        head = lax.slice_in_dim(cells, 0, width, axis=dim)
        tail = lax.slice_in_dim(cells, cells.shape[dim] - width, cells.shape[dim], axis=dim)
        cells = jnp.concatenate(
            [
                lax.ppermute(tail, axis, [(i, (i + 1) % count) for i in range(count)]),
                cells,
                lax.ppermute(head, axis, [((i + 1) % count, i) for i in range(count)]),
            ],
            axis=dim,
        )
    return cells


def split_up(value, dim, size):
    lengths = value.shape
    pieces = value.reshape(*lengths[:dim], size, lengths[dim] // size, *lengths[dim + 1 :])
    return jnp.moveaxis(pieces, dim, 0)


def sent_and_summed(value, axis, dim):
    size = lax.axis_size(axis)
    pieces = lax.all_to_all(split_up(value, dim, size), axis, 0, 0, tiled=True)
    return jnp.sum(pieces, axis=0)


def sent_to_all(value, axis):
    size = lax.axis_size(axis)
    return lax.all_to_all(
        jnp.broadcast_to(value[None], (size, *value.shape)), axis, 0, 0, tiled=True
    )


def of_everyone(value, axis):
    return sent_to_all(value, axis).sum(axis=0)


def packed_total(arrays, axis):
    vector, at, done = (jnp.concatenate([a.reshape(-1) for a in arrays]), 0, [])
    subtotal = of_everyone(vector, axis)
    for a in arrays:
        done.append(subtotal[at : at + a.size].reshape(a.shape))
        at += a.size
    return tuple(done)


def turned_gather(arrays, axis, dims):
    turned = [jnp.moveaxis(a, dim, 0) for a, dim in zip(arrays, dims)]
    both = jnp.concatenate([t.reshape(len(t), -1) for t in turned], axis=1)
    filled, at, done = (lax.all_gather(both, axis, axis=0, tiled=True), 0, [])
    for t, dim in zip(turned, dims):
        section = filled[:, at : at + t[0].size].reshape(-1, *t.shape[1:])
        done.append(jnp.moveaxis(section, 0, dim))
        at += t[0].size
    return tuple(done)


def correlate(padded, along_x, along_y):
    row_count = padded.shape[-2] - 2
    col_count = padded.shape[-1] - 2
    partial_x = None
    for offset in range(3):
        if along_x[offset] != 0.0:
            weighted = along_x[offset] * padded[..., offset : offset + row_count, :]
            partial_x = weighted if partial_x is None else partial_x + weighted
    running = None
    for offset in range(3):
        if along_y[offset] != 0.0:
            weighted = along_y[offset] * partial_x[..., offset : offset + col_count]
            running = weighted if running is None else running + weighted
    return running


def mirrored(padded, along_x, along_y):
    return correlate(padded, along_x[::-1], along_y[::-1])


def strains(padded):
    along_u, along_v, along_w = (padded[0], padded[1], padded[2])
    return jnp.stack(
        [
            correlate(along_u, BASIS_SLOPE, BASIS_VALUE),
            correlate(along_v, BASIS_VALUE, BASIS_SLOPE)
            + HOOP_CURVATURE * correlate(along_w, BASIS_VALUE, BASIS_VALUE),
            correlate(along_u, BASIS_VALUE, BASIS_SLOPE)
            + correlate(along_v, BASIS_SLOPE, BASIS_VALUE),
            -correlate(along_w, BASIS_CURVE, BASIS_VALUE),
            -correlate(along_w, BASIS_VALUE, BASIS_CURVE),
            -2.0 * correlate(along_w, BASIS_SLOPE, BASIS_SLOPE),
        ]
    )


def forces(spread):
    force_u = mirrored(spread[0], BASIS_SLOPE, BASIS_VALUE) + mirrored(
        spread[2], BASIS_VALUE, BASIS_SLOPE
    )
    force_v = mirrored(spread[1], BASIS_VALUE, BASIS_SLOPE) + mirrored(
        spread[2], BASIS_SLOPE, BASIS_VALUE
    )
    force_w = (
        HOOP_CURVATURE * mirrored(spread[1], BASIS_VALUE, BASIS_VALUE)
        - mirrored(spread[3], BASIS_CURVE, BASIS_VALUE)
        - mirrored(spread[4], BASIS_VALUE, BASIS_CURVE)
        - 2.0 * mirrored(spread[5], BASIS_SLOPE, BASIS_SLOPE)
    )
    return jnp.stack([force_u, force_v, force_w])


def apply_layup(stiffness_map, strain):
    running = stiffness_map[:, 0] * strain[0]
    for column in range(1, 6):
        running = running + stiffness_map[:, column] * strain[column]
    return running


def outer_product(left, right):
    return lax.dot_general(
        left, right, (((1,), (1,)), ((), ())), preferred_element_type=jnp.float32
    )


def forward_mlp(inputs, w_first, w_mid, w_last):
    hidden_layer = jnp.tanh(jnp.dot(w_first, inputs, preferred_element_type=jnp.float32)).astype(
        jnp.bfloat16
    )
    activations = [hidden_layer]
    for layer_index in range(w_mid.shape[0]):
        hidden_layer = jnp.tanh(
            jnp.dot(w_mid[layer_index], hidden_layer, preferred_element_type=jnp.float32)
        ).astype(jnp.bfloat16)
        activations.append(hidden_layer)
    return (jnp.dot(w_last, hidden_layer, preferred_element_type=jnp.float32), activations)


def backward_mlp(inputs, activations, upstream, w_mid, w_last):
    grad_last = outer_product(upstream, activations[-1])
    signal = jnp.dot(w_last.T, upstream, preferred_element_type=jnp.float32)
    derivative = (signal * (1.0 - jnp.square(activations[-1].astype(jnp.float32)))).astype(
        jnp.bfloat16
    )
    mid_grads = []
    for layer_index in range(w_mid.shape[0] - 1, -1, -1):
        mid_grads.append(outer_product(derivative, activations[layer_index]))
        signal = jnp.dot(w_mid[layer_index].T, derivative, preferred_element_type=jnp.float32)
        derivative = (
            signal * (1.0 - jnp.square(activations[layer_index].astype(jnp.float32)))
        ).astype(jnp.bfloat16)
    grad_first = outer_product(derivative, inputs)
    return (grad_first, jnp.stack(mid_grads[::-1]), grad_last)


def two_products(remainder, mapped):
    return (
        by_axis(jnp.sum(remainder * remainder), PATCH_SUB),
        by_axis(jnp.sum(remainder * mapped), PATCH_SUB),
    )


def careful(displacement, load, foundation, layup, layup_stiffness, w_first, w_mid, w_last):
    layup_count = layup_stiffness.shape[0]

    def coefficients(layup_ids):
        onehot = (
            layup_ids[None] == jnp.arange(layup_count, dtype=jnp.int32)[:, None, None]
        ).astype(jnp.float32)
        return jnp.einsum("lab,lxy->abxy", layup_stiffness, onehot, precision=lax.Precision.HIGHEST)

    stiffness_map = coefficients(layup)
    wide_ids = padded_2(layup, ((PATCH, 0), (SUB, 1)), 1)
    stiffness_wide = coefficients(wide_ids)

    def operate(search):
        padded = padded_2(search, ((PATCH, 1), (SUB, 2)), 2)
        return forces(apply_layup(stiffness_wide, strains(padded))) + foundation * search

    padded = padded_2(displacement, ((PATCH, 1), (SUB, 2)), 1)
    strain = strains(padded)
    inputs = strain.reshape(6, -1).astype(jnp.bfloat16)
    learned, activations = forward_mlp(inputs, w_first, w_mid, w_last)
    stress = apply_layup(stiffness_map, strain) + learned.reshape(strain.shape)
    spread = padded_2(stress, ((PATCH, 1), (SUB, 2)), 1)
    residual = forces(spread) + foundation * displacement - load
    adjoint = jnp.zeros_like(residual)
    remainder = residual
    mapped = operate(remainder)
    norm_now, curved = two_products(remainder, mapped)
    step_size = norm_now / curved
    direction, mapped_dir = (remainder, mapped)
    for step_index in range(ITERS):
        adjoint = adjoint + step_size * direction
        remainder = remainder - step_size * mapped_dir
        if step_index + 1 < ITERS:
            mapped = operate(remainder)
            norm_next, curved = two_products(remainder, mapped)
            beta_ratio = norm_next / norm_now
            step_size = norm_next / (curved - beta_ratio * norm_next / step_size)
            direction = remainder + beta_ratio * direction
            mapped_dir = mapped + beta_ratio * mapped_dir
            norm_now = norm_next
    cycle = padded_2(adjoint, ((PATCH, 1), (SUB, 2)), 1)
    upstream = strains(cycle).reshape(6, -1).astype(jnp.bfloat16)
    grad_first, grad_mid, grad_last = backward_mlp(inputs, activations, upstream, w_mid, w_last)
    shares = (
        sent_and_summed(grad_first, SUB, 0),
        sent_and_summed(grad_mid, SUB, 1),
        sent_and_summed(grad_last, SUB, 1),
    )
    crossed = packed_total((shares[0], shares[1], shares[2]), PATCH)
    totals = turned_gather((crossed[0], crossed[1], crossed[2]), SUB, (0, 1, 1))
    return (residual, adjoint, totals[0], totals[1], totals[2])


ROWS = 24
SEGS = 24
LANES = 128
OWN = 8
TILES = 16
STEP = 512
TRUST = 400.0
MESH = pl.DeviceIdType.MESH
PAIRS = [(a, b) for a in range(6) for b in range(a, 6)]
SPOT = {pair: k for k, pair in enumerate(PAIRS)}


def flat(ref):
    lead, mid, lanes = ref.shape
    return ref.reshape(lead * mid, lanes)


def column(ref, fields, field, row, segment):
    return flat(ref).at[pl.ds((row * fields + field) * SEGS + segment, 8, stride=fields * SEGS), :]


def lane_of():
    return lax.broadcasted_iota(jnp.int32, (SEGS, LANES), 1)


def after(field, lane):
    turned = pltpu.roll(field, LANES - 1, 1)
    return jnp.where(lane == LANES - 1, pltpu.roll(turned, SEGS - 1, 0), turned)


def before(field, lane):
    turned = pltpu.roll(field, 1, 1)
    return jnp.where(lane == 0, pltpu.roll(turned, 1, 0), turned)


def along_columns(read, y_ref, first, last):
    lane = lane_of()

    def body(e, carry):
        u, v, w = read(e)
        at = e * 7
        for k, field in enumerate((u, v, w)):
            ahead, behind = after(field, lane), before(field, lane)
            both = ahead + behind
            y_ref[at + 2 * k] = 0.75 * field + 0.125 * both
            y_ref[at + 2 * k + 1] = 0.5 * (ahead - behind)
            if k == 2:
                y_ref[at + 6] = both - 2.0 * field
        return carry

    lax.fori_loop(first, last, body, 0, unroll=2)


def strains_at(y_ref, e):
    at = e * 7

    def three(k):
        return y_ref[at - 7 + k], y_ref[at + k], y_ref[at + 7 + k]

    def value(k):
        m, c, p = three(k)
        return 0.75 * c + 0.125 * (p + m)

    def slope(k):
        return 0.5 * (y_ref[at + 7 + k] - y_ref[at - 7 + k])

    m, c, p = three(4)
    pair = p + m
    return [
        slope(0),
        value(3) + HOOP_CURVATURE * (0.75 * c + 0.125 * pair),
        value(1) + slope(2),
        2.0 * c - pair,
        -value(6),
        y_ref[at - 7 + 5] - y_ref[at + 7 + 5],
    ]


def laminate(c_ref, e, strain):
    at = e * 21
    total = [None] * 6
    for (a, b), k in SPOT.items():
        c = c_ref[at + k]
        term = c * strain[b]
        total[a] = term if total[a] is None else total[a] + term
        if a != b:
            term = c * strain[a]
            total[b] = term if total[b] is None else total[b] + term
    return total


def forces_at(s_ref, e, lane):
    at = e * 6

    def three(k):
        return s_ref[at - 6 + k], s_ref[at + k], s_ref[at + 6 + k]

    def value(k):
        m, c, p = three(k)
        return 0.75 * c + 0.125 * (p + m)

    def slope(k):
        return 0.5 * (s_ref[at - 6 + k] - s_ref[at + 6 + k])

    def spread(here, behind, ahead):
        return here + before(behind, lane) + after(ahead, lane)

    a, b = slope(0), value(2)
    force_u = spread(0.75 * a, 0.125 * a + 0.5 * b, 0.125 * a - 0.5 * b)
    a, b = slope(2), value(1)
    force_v = spread(0.75 * a, 0.125 * a + 0.5 * b, 0.125 * a - 0.5 * b)
    m, c, p = three(3)
    a = HOOP_CURVATURE * b - ((m + p) - 2.0 * c)
    d = value(4)
    half = slope(5)
    base = 0.125 * a - d
    force_w = spread(0.75 * a + 2.0 * d, base - half, base + half)
    return force_u, force_v, force_w


def fused(
    disp_in, load_in, found_in, lay_in, stiff, w1t, wm, wl,
    res_o, adj_o, gf_o, gm_o, gl_o, trust_o,
    disp, load, found, lay, in_s, dsp, aux, ids, lod, edge_a, edge_c, got_a, got_c, y_ref, s_ref, c_ref, x_ref, l_ref, u_ref, h_ref,
    v0, v1, v2, v3, wmt, acc_m, acc_s,
    d_out, d_in, d_mid, d_in2, e_out, e_in, e_mid, e_in2, e_end, e_in3,
    g_out, g_in, g_mid, g_in2, g_end, g_in3,
    a_s, a_r, c_s, c_r, d1_s, d1_r, d2_s, d2_r, e1_s, e1_r, e2_s, e2_r, e3_s, e3_r,
    g1_s, g1_r, g2_s, g2_r, g3_s, g3_r,
):
    me_p, me_s = lax.axis_index("patch"), lax.axis_index("sub")
    count_p, count_s = lax.axis_size("patch"), lax.axis_size("sub")

    def place(dp, ds):
        return {"patch": lax.rem(me_p + dp, count_p), "sub": lax.rem(me_s + ds, count_s)}

    up, down = count_p - 1, 1
    left, right = count_s - 1, 1
    greeted = [(0, k) for k in range(1, count_s)] + [(k, 0) for k in range(1, count_p)]
    greeted += [(a, b) for a in (up, down) for b in (left, right)]
    barrier = pltpu.get_barrier_semaphore()
    for dp, ds in greeted:
        pl.semaphore_signal(barrier, inc=1, device_id=place(dp, ds), device_id_type=MESH)

    arriving = [
        pltpu.make_async_copy(source, held, in_s.at[k])
        for k, (source, held) in enumerate(((disp_in, disp), (lay_in, lay), (found_in, found), (load_in, load)))
    ]
    for copy in arriving:
        copy.start()
    for copy in arriving[:3]:
        copy.wait()

    for t in range(TILES):
        cut = pl.ds(t * LANES, LANES)
        for f in range(3):
            column(dsp, 3, f, OWN, 8 + t)[...] = disp[f, :, cut]
        column(ids, 1, 0, OWN, 8 + t)[...] = lay[:, cut].astype(jnp.float32)
    ends = ((0, pl.ds(0, LANES)), (1, pl.ds((TILES - 1) * LANES, LANES)))
    for side, cut in ends:
        for f in range(3):
            edge_a[side, f] = disp[f, :, cut]
            edge_a[side, 4 + f] = found[f, :, cut]
        edge_a[side, 3] = lay[:, cut].astype(jnp.float32)

    pl.semaphore_wait(barrier, len(greeted))

    def send(src, dst, sent, received, to):
        return pltpu.make_async_remote_copy(
            src_ref=src, dst_ref=dst, send_sem=sent, recv_sem=received, device_id=to, device_id_type=MESH
        )

    def rows_to(ref, fields, near, far, sent, received, first):
        own, n = pl.ds(OWN, TILES), (far - near) * fields
        below = send(
            ref.at[pl.ds((16 - far) * fields, n), own, :],
            ref.at[pl.ds((8 - far) * fields, n), own, :],
            sent.at[first], received.at[first], place(down, 0),
        )
        above = send(
            ref.at[pl.ds((8 + near) * fields, n), own, :],
            ref.at[pl.ds((16 + near) * fields, n), own, :],
            sent.at[first + 1], received.at[first + 1], place(up, 0),
        )
        return [below, above]

    heading = ((0, right, 1), (0, left, 0), (down, right, 1), (down, left, 0), (up, right, 1), (up, left, 0))

    def edges_to(edge, got, fields, sent, received, first):
        return [
            send(edge.at[side, fields], got.at[k, fields], sent.at[first + k], received.at[first + k], place(dp, ds))
            for k, (dp, ds, side) in reversed(list(enumerate(heading)))
        ]

    def start(copies):
        for copy in copies:
            copy.start()

    landing = ((7, 8), (0, 8), (7, 0), (0, 0), (7, 16), (0, 16))

    first_a = (
        edges_to(edge_a, got_a, pl.ds(0, 4), a_s, a_r, 2)
        + rows_to(dsp, 3, 0, 2, a_s, a_r, 0)
        + rows_to(ids, 1, 0, 1, a_s, a_r, 8)
    )
    start(first_a)
    arriving[3].wait()
    for t in range(TILES):
        cut = pl.ds(t * LANES, LANES)
        for f in range(3):
            column(aux, 3, f, OWN, 8 + t)[...] = found[f, :, cut]
            column(lod, 3, f, 0, 8 + t)[...] = load[f, :, cut]
    for k in range(3):
        wmt[k] = wm[k].T
    w1 = w1t[...].T
    wlt = wl[...].T

    def choose_row(e, carry):
        kind = ids[e].astype(jnp.int32)
        low, middle, high = (kind & 1) == 1, (kind & 2) == 2, (kind & 4) == 4
        for k, (a, b) in enumerate(PAIRS):
            p = [jnp.where(low, stiff[a, 2 * q + 1, b], stiff[a, 2 * q, b]) for q in range(4)]
            c_ref[e * 21 + k] = jnp.where(
                high, jnp.where(middle, p[3], p[2]), jnp.where(middle, p[1], p[0])
            )
        return carry

    for copy in first_a:
        copy.wait()
    second_a = (
        rows_to(aux, 3, 0, 5, a_s, a_r, 10)
        + rows_to(ids, 1, 1, 6, a_s, a_r, 12)
        + edges_to(edge_a, got_a, pl.ds(4, 3), a_s, a_r, 14)
    )
    start(second_a)
    for k, (segment, row) in enumerate(landing):
        for f in range(3):
            column(dsp, 3, f, row, segment)[...] = got_a[k, f]
        column(ids, 1, 0, row, segment)[...] = got_a[k, 3]

    lane = lane_of()
    along_columns(lambda e: [dsp[e * 3 + f] for f in range(3)], y_ref, 6, 18)

    def strain_row(r, carry):
        e = r + 7
        strain = strains_at(y_ref, e)
        for k in range(6):
            s_ref[e * 6 + k] = strain[k]
            flat(x_ref)[pl.ds(r * (SEGS * 8) + k, SEGS, stride=8), :] = strain[k]
        return carry

    lax.fori_loop(0, 10, strain_row, 0)
    tile_lane = lax.broadcasted_iota(jnp.int32, (8, LANES), 1)
    beside = 10 * SEGS
    packed = jnp.zeros((8, LANES), jnp.float32)
    for r in range(10):
        ends_of = jnp.where(tile_lane < 64, x_ref[r * SEGS], x_ref[r * SEGS + 7])
        turned = pltpu.roll(ends_of, 2 * r + 1, 1)
        packed = jnp.where((tile_lane == 2 * r) | (tile_lane == 2 * r + 1), turned, packed)
    x_ref[beside] = packed

    def operand(ref, at, width):
        tiles = [ref[at + q] for q in range(width // LANES)]
        return jnp.concatenate(tiles, axis=1)[:6].astype(jnp.bfloat16)

    def learn(parts):
        for at, slot, first, width in parts:
            h_ref[slot, :, pl.ds(first, width)] = jnp.tanh(
                jnp.dot(w1, operand(x_ref, at, width), preferred_element_type=jnp.float32)
            ).astype(jnp.bfloat16)
        for k in range(3):
            for at, slot, first, width in parts:
                cut = pl.ds(first, width)
                h_ref[slot + k + 1, :, cut] = jnp.tanh(
                    jnp.dot(wm[k], h_ref[slot + k, :, cut], preferred_element_type=jnp.float32)
                ).astype(jnp.bfloat16)
        for at, slot, first, width in parts:
            out = jnp.dot(wl[...], h_ref[slot + 3, :, pl.ds(first, width)], preferred_element_type=jnp.float32)
            for q in range(width // LANES):
                l_ref[at + q, 0:6, :] = out[:, q * LANES : (q + 1) * LANES]

    def row_parts(r, slot):
        return [
            (r * SEGS + 8 + c * (STEP // LANES), slot, c * STEP, STEP) for c in range(2048 // STEP)
        ]

    def stress_row(r):
        e = r + 7
        choose_row(e, 0)
        stress = laminate(c_ref, e, [s_ref[e * 6 + k] for k in range(6)])
        for k in range(6):
            s_ref[e * 6 + k] = stress[k] + flat(l_ref)[pl.ds(r * (SEGS * 8) + k, SEGS, stride=8), :]

    def residual_row(e):
        force = forces_at(s_ref, e, lane)
        for f in range(3):
            v0[e * 3 + f] = force[f] + aux[e * 3 + f] * dsp[e * 3 + f] - lod[(e - 8) * 3 + f]

    def residual_to(e):
        own, row = pl.ds(OWN, TILES), v0.at[pl.ds(e * 3, 3), pl.ds(OWN, TILES), :]
        return [
            send(row, v0.at[pl.ds((e - 8) * 3, 3), own, :], c_s.at[e - 2], c_r.at[e - 2], place(down, 0)),
            send(row, v0.at[pl.ds((e + 8) * 3, 3), own, :], c_s.at[e + 6], c_r.at[e + 6], place(up, 0)),
        ]

    learn([(beside, 32, 0, LANES)] + row_parts(0, 36))
    for r in range(10):
        turned = pltpu.roll(l_ref[beside], LANES - 1 - 2 * r, 1)
        l_ref[r * SEGS] = turned
        l_ref[r * SEGS + 7] = turned
    for r in (1, 2):
        stress_row(r - 1)
        learn(row_parts(r, (r - 1) * 4))

    def pipelined_row(r, carry):
        @pl.when(r > 3)
        def _():
            start(residual_to(r + 4))

        stress_row(r - 1)
        residual_row(r + 5)
        learn(row_parts(r, (r - 1) * 4))
        return carry

    lax.fori_loop(3, 10, pipelined_row, 0)
    start(residual_to(14))
    stress_row(9)
    residual_row(15)
    start(residual_to(15))
    for side, t in ((0, 0), (1, TILES - 1)):
        for f in range(3):
            edge_c[side, f] = column(v0, 3, f, OWN, 8 + t)[...]
    moves_c = edges_to(edge_c, got_c, pl.ds(0, 3), c_s, c_r, 0)
    start(moves_c)
    for copy in second_a:
        copy.wait()
    for k, (segment, row) in enumerate(landing):
        for f in range(3):
            column(aux, 3, f, row, segment)[...] = got_a[k, 4 + f]
    lax.fori_loop(2, 7, choose_row, 0)
    lax.fori_loop(17, 22, choose_row, 0)
    for t in range(TILES):
        for f in range(3):
            res_o[f, :, pl.ds(t * LANES, LANES)] = column(v0, 3, f, OWN, 8 + t)[...]
    for copy in moves_c:
        copy.wait()
    for e in range(8, 16):
        for copy in residual_to(e):
            copy.wait()
    for k, (segment, row) in enumerate(landing):
        for f in range(3):
            column(v0, 3, f, row, segment)[...] = got_c[k, f]

    def mean(k):
        total = stiff[k, 0, k]
        for q in range(1, 8):
            total = total + stiff[k, q, k]
        return total * 0.125

    half = 1.0 + 8.0 * jnp.maximum(mean(3), mean(4))
    center = jnp.full((1, LANES), half, jnp.float32)
    inverse = 1.0 / center

    def apply_stiffness(v, older, out, first, last):
        along_columns(lambda e: [v[e * 3 + f] for f in range(3)], y_ref, first - 2, last + 2)

        def body(e, carry):
            stress = laminate(c_ref, e, strains_at(y_ref, e))
            for k in range(6):
                s_ref[e * 6 + k] = stress[k]
            return carry

        lax.fori_loop(first - 1, last + 1, body, 0, unroll=2)

        def finish(e, carry):
            force = forces_at(s_ref, e, lane)
            for f in range(3):
                here = v[e * 3 + f]
                image = force[f] + aux[e * 3 + f] * here
                if older is None:
                    out[e * 3 + f] = inverse * image - here
                else:
                    out[e * 3 + f] = (2.0 * inverse) * image - 2.0 * here - older[e * 3 + f]
            return carry

        lax.fori_loop(first, last, finish, 0, unroll=2)

    apply_stiffness(v0, None, v1, 3, 21)
    apply_stiffness(v1, v0, v2, 5, 19)
    apply_stiffness(v2, v1, v3, 7, 17)
    along_columns(lambda e: [v3[e * 3 + f] for f in range(3)], y_ref, 7, 17)

    def folded(field):
        return field[8:16] + field[16:24]

    def sums_row(e, totals):
        strain = strains_at(y_ref, e)
        stress = laminate(c_ref, e, strain)
        energy = strain[0] * stress[0]
        for k in range(1, 6):
            energy = energy + strain[k] * stress[k]
        totals = list(totals)
        for f in range(3):
            a, b, c, d = v0[e * 3 + f], v1[e * 3 + f], v2[e * 3 + f], v3[e * 3 + f]
            energy = energy + aux[e * 3 + f] * (d * d)
            for k, product in enumerate((a * a, a * b, b * b, b * c, c * c, c * d, d * d)):
                totals[k] = totals[k] + folded(product)
        totals[7] = totals[7] + folded(energy)
        return tuple(totals)

    totals = lax.fori_loop(8, 16, sums_row, tuple(jnp.zeros((8, LANES), jnp.float32) for _ in range(8)))
    d_out[...] = jnp.concatenate([jnp.sum(t, axis=0, keepdims=True) for t in totals], axis=0)

    def shared(source, slots, sent, received, count, mine, spot, piece=None):
        copies = []
        for k in range(1, count):
            src = source if piece is None else source.at[lax.rem(mine + k, count)]
            copies.append(send(src, slots.at[mine], sent.at[k], received.at[mine], spot(k)))
        start(copies)
        own = source if piece is None else source.at[mine]
        slots[mine] = own[...]

        def finish():
            for k in range(1, count):
                other = lax.rem(mine + k, count)
                src = source if piece is None else source.at[other]
                send(src, slots.at[other], sent.at[k], received.at[other], spot(k)).wait()

        return finish

    def summed(slots, count):
        total = slots[0]
        for k in range(1, count):
            total = total + slots[k]
        return total

    by_sub, by_patch = (lambda k: place(0, k)), (lambda k: place(k, 0))
    shared(d_out, d_in, d1_s, d1_r, count_s, me_s, by_sub)()
    d_mid[...] = summed(d_in, count_s)
    shared(d_mid, d_in2, d2_s, d2_r, count_p, me_p, by_patch)()
    everyone = jnp.sum(summed(d_in2, count_p), axis=1, keepdims=True)
    n = [jnp.broadcast_to(everyone[k : k + 1], (1, LANES)) for k in range(8)]
    n34 = (2.0 * inverse) * n[7] - 2.0 * n[6] - n[5]
    m = [n[0], n[1]]
    for k in (2, 3, 4, 5, 6):
        m.append(2.0 * n[k] - m[k % 2])
    m.append(2.0 * n34 - m[1])

    def gram(i, j):
        return 0.5 * (m[i + j] + m[abs(i - j)])

    def form(x, y):
        total, size = None, None
        for i, a in enumerate(x):
            for j, b in enumerate(y):
                term = a * b * gram(i, j)
                total = term if total is None else total + term
                size = jnp.abs(term) if size is None else size + jnp.abs(term)
        return total, size / total

    def image_of(x):
        zero = jnp.zeros((1, LANES), jnp.float32)
        out = [center * a for a in x] + [zero]
        for j, a in enumerate(x):
            if j == 0:
                out[1] = out[1] + center * a
            else:
                out[j + 1] = out[j + 1] + (0.5 * center) * a
                out[j - 1] = out[j - 1] + (0.5 * center) * a
        return out

    one = jnp.ones((1, LANES), jnp.float32)
    zero = jnp.zeros((1, LANES), jnp.float32)
    rest, way, found_y, norm = [one], [one], [zero] * 4, m[0]
    worst = one
    for step in range(ITERS):
        image = image_of(way)
        curved, spread = form(way, image)
        worst = jnp.where(spread <= TRUST, worst, 2.0 * TRUST * one)
        alpha = norm / curved
        found_y = [found_y[k] + alpha * way[k] if k < len(way) else found_y[k] for k in range(4)]
        if step + 1 < ITERS:
            rest = [(rest[k] if k < len(rest) else zero) - alpha * image[k] for k in range(len(image))]
            fresh, spread = form(rest, rest)
            worst = jnp.where(spread <= TRUST, worst, 2.0 * TRUST * one)
            beta = fresh / norm
            way = [rest[k] + (beta * way[k] if k < len(way) else zero) for k in range(len(rest))]
            norm = fresh
    trust_o[0, 0] = worst[0, 0]

    def adjoint_row(e, carry):
        for f in range(3):
            at = e * 3 + f
            v0[at] = found_y[0] * v0[at] + found_y[1] * v1[at] + found_y[2] * v2[at] + found_y[3] * v3[at]
        return carry

    lax.fori_loop(7, 17, adjoint_row, 0)
    for t in range(TILES):
        for f in range(3):
            adj_o[f, :, pl.ds(t * LANES, LANES)] = column(v0, 3, f, OWN, 8 + t)[...]
    along_columns(lambda e: [v0[e * 3 + f] for f in range(3)], y_ref, 7, 17)

    def upstream_row(e, carry):
        strain = strains_at(y_ref, e)
        for k in range(6):
            flat(u_ref)[pl.ds((e - 8) * (SEGS * 8) + k, SEGS, stride=8), :] = strain[k]
        return carry

    lax.fori_loop(8, 16, upstream_row, 0)

    acc_m[...] = jnp.zeros_like(acc_m)
    acc_s[...] = jnp.zeros_like(acc_s)

    def derive(weights, signal_of, slot):
        for c in range(2048 // STEP):
            cut = pl.ds(c * STEP, STEP)
            h = h_ref[slot, :, cut].astype(jnp.float32)
            signal = jnp.dot(weights, signal_of(c, cut), preferred_element_type=jnp.float32)
            h_ref[slot, :, cut] = (signal * (1.0 - jnp.square(h))).astype(jnp.bfloat16)

    def back_last(r, carry):
        slot = r * 4 + 3
        u = operand(u_ref, r * SEGS + 8, 2048)
        acc_s[0:6] += outer_product(u, h_ref[slot])
        derive(wlt, lambda c, cut: u[:, c * STEP : (c + 1) * STEP], slot)
        return carry

    def back_mid(k):
        def body(r, carry):
            slot = r * 4 + k
            acc_m[k] += outer_product(h_ref[slot + 1], h_ref[slot])
            derive(wmt[k], lambda c, cut: h_ref[slot + 1, :, cut], slot)
            return carry

        lax.fori_loop(0, 8, body, 0)

    def back_first(r, carry):
        acc_s[8:14] += outer_product(operand(x_ref, (r + 1) * SEGS + 8, 2048), h_ref[r * 4])
        return carry

    lax.fori_loop(0, 8, back_last, 0)
    back_mid(2)
    back_mid(1)
    for k in range(16):
        e_out[k, 0:8, :] = acc_m[1, 8 * k : 8 * k + 8]
        e_out[k, 8:16, :] = acc_m[2, 8 * k : 8 * k + 8]
    finish_e1 = shared(e_out, e_in, e1_s, e1_r, count_s, me_s, by_sub, piece=True)
    back_mid(0)
    lax.fori_loop(0, 8, back_first, 0)
    for k in range(16):
        g_out[k, 0:8, :] = acc_m[0, 8 * k : 8 * k + 8]
        g_out[k, 8:9, :] = acc_s[k : k + 1]
    finish_g1 = shared(g_out, g_in, g1_s, g1_r, count_s, me_s, by_sub, piece=True)
    finish_e1()
    e_mid[...] = summed(e_in, count_s)
    finish_e2 = shared(e_mid, e_in2, e2_s, e2_r, count_p, me_p, by_patch)
    finish_g1()
    g_mid[...] = summed(g_in, count_s)
    finish_g2 = shared(g_mid, g_in2, g2_s, g2_r, count_p, me_p, by_patch)
    finish_e2()
    e_end[...] = summed(e_in2, count_p)
    finish_e3 = shared(e_end, e_in3, e3_s, e3_r, count_s, me_s, by_sub)
    finish_g2()
    g_end[...] = summed(g_in2, count_p)
    finish_g3 = shared(g_end, g_in3, g3_s, g3_r, count_s, me_s, by_sub)
    finish_e3()
    for k in range(16):
        gm_o[1, 8 * k : 8 * k + 8] = e_in3[k, 0:8, :]
        gm_o[2, 8 * k : 8 * k + 8] = e_in3[k, 8:16, :]
    finish_g3()
    for k in range(16):
        gm_o[0, 8 * k : 8 * k + 8] = g_in3[k, 0:8, :]
    for k in range(6):
        gl_o[k : k + 1] = g_in3[k, 8:9, :]
        gf_o[k : k + 1] = g_in3[8 + k, 8:9, :]


def per_device(displacement, load, foundation, layup, layup_stiffness, w_first, w_mid, w_last):
    vmem = pl.BlockSpec(memory_space=pltpu.VMEM)
    smem = pl.BlockSpec(memory_space=pltpu.SMEM)
    f32, bf16 = jnp.float32, jnp.bfloat16

    def rows(fields, count=ROWS):
        return pltpu.VMEM((count * fields, SEGS, LANES), f32)

    dma = pltpu.SemaphoreType.DMA
    out = pl.pallas_call(
        fused,
        out_shape=[
            jax.ShapeDtypeStruct(displacement.shape, f32),
            jax.ShapeDtypeStruct(displacement.shape, f32),
            jax.ShapeDtypeStruct((6, 128), f32),
            jax.ShapeDtypeStruct((3, 128, 128), f32),
            jax.ShapeDtypeStruct((6, 128), f32),
            jax.ShapeDtypeStruct((1, 1), f32),
        ],
        in_specs=[pl.BlockSpec(memory_space=pl.ANY)] * 4 + [smem] + [vmem] * 3,
        out_specs=[vmem] * 5 + [smem],
        scratch_shapes=[
            pltpu.VMEM(displacement.shape, f32), pltpu.VMEM(displacement.shape, f32),
            pltpu.VMEM(displacement.shape, f32), pltpu.VMEM(layup.shape, jnp.int32), dma((4,)),
            rows(3), rows(3), rows(1), rows(3, 8),
            pltpu.VMEM((2, 7, 8, LANES), f32), pltpu.VMEM((2, 3, 8, LANES), f32),
            pltpu.VMEM((6, 7, 8, LANES), f32), pltpu.VMEM((6, 3, 8, LANES), f32),
            rows(7), rows(6), rows(21),
            pltpu.VMEM((11 * SEGS, 8, LANES), f32),
            pltpu.VMEM((11 * SEGS, 8, LANES), f32),
            pltpu.VMEM((8 * SEGS, 8, LANES), f32),
            pltpu.VMEM((10 * 4, 128, 2048), bf16),
            rows(3), rows(3), rows(3), rows(3),
            pltpu.VMEM((3, 128, 128), bf16),
            pltpu.VMEM((3, 128, 128), f32), pltpu.VMEM((16, 128), f32),
            pltpu.VMEM((8, LANES), f32), pltpu.VMEM((16, 8, LANES), f32),
            pltpu.VMEM((8, LANES), f32), pltpu.VMEM((16, 8, LANES), f32),
        ] + [
            pltpu.VMEM(shape, f32)
            for n in (16, 9)
            for shape in [(16, n, LANES), (16, n, LANES), (n, LANES)] + [(16, n, LANES), (n, LANES), (16, n, LANES)]
        ] + [
            dma((20,)), dma((20,)), dma((22,)), dma((22,)),
        ] + [dma((16,)) for _ in range(16)],
        compiler_params=pltpu.CompilerParams(
            collective_id=0, has_side_effects=True, vmem_limit_bytes=46 << 20
        ),
        name="adjoint_step",
    )(
        displacement, load, foundation, layup, layup_stiffness.transpose(1, 0, 2), w_first.T, w_mid, w_last
    )
    fast, trust = (out[0], out[1], out[2].T, out[3], out[4]), out[5][0, 0]
    operands = (displacement, load, foundation, layup, layup_stiffness, w_first, w_mid, w_last)
    return lax.cond(trust <= TRUST, lambda: fast, lambda: careful(*operands))


def solution(mesh):
    return jax.shard_map(
        per_device,
        mesh=mesh,
        in_specs=(
            P(None, "patch", "sub"),
            P(None, "patch", "sub"),
            P(None, "patch", "sub"),
            P("patch", "sub"),
            P(),
            P(),
            P(),
            P(),
        ),
        out_specs=(P(None, "patch", "sub"), P(None, "patch", "sub"), P(), P(), P()),
        check_vma=False,
    )
```

```python
import functools

import jax
import jax.numpy as jnp
from jax import lax
from jax.experimental import pallas as pl
from jax.experimental.pallas import tpu as pltpu
from jax.sharding import PartitionSpec as P

ITERS = 4
PATCH_SUB = ("patch", "sub")
PATCH = "patch"
SUB = "sub"


BASIS_VALUE = (0.125, 0.75, 0.125)
BASIS_SLOPE = (-0.5, 0.0, 0.5)
BASIS_CURVE = (1.0, -2.0, 1.0)
HOOP_CURVATURE = 0.25


def by_axis(value, axes):
    return lax.psum(value, axes)


def padded_2(cells, sides, width):
    for axis, dim in sides:
        count = lax.axis_size(axis)
        head = lax.slice_in_dim(cells, 0, width, axis=dim)
        tail = lax.slice_in_dim(cells, cells.shape[dim] - width, cells.shape[dim], axis=dim)
        cells = jnp.concatenate(
            [
                lax.ppermute(tail, axis, [(i, (i + 1) % count) for i in range(count)]),
                cells,
                lax.ppermute(head, axis, [((i + 1) % count, i) for i in range(count)]),
            ],
            axis=dim,
        )
    return cells


def split_up(value, dim, size):
    lengths = value.shape
    pieces = value.reshape(*lengths[:dim], size, lengths[dim] // size, *lengths[dim + 1 :])
    return jnp.moveaxis(pieces, dim, 0)


def sent_and_summed(value, axis, dim):
    size = lax.axis_size(axis)
    pieces = lax.all_to_all(split_up(value, dim, size), axis, 0, 0, tiled=True)
    return jnp.sum(pieces, axis=0)


def sent_to_all(value, axis):
    size = lax.axis_size(axis)
    return lax.all_to_all(
        jnp.broadcast_to(value[None], (size, *value.shape)), axis, 0, 0, tiled=True
    )


def of_everyone(value, axis):
    return sent_to_all(value, axis).sum(axis=0)


def packed_total(arrays, axis):
    vector, at, done = (jnp.concatenate([a.reshape(-1) for a in arrays]), 0, [])
    subtotal = of_everyone(vector, axis)
    for a in arrays:
        done.append(subtotal[at : at + a.size].reshape(a.shape))
        at += a.size
    return tuple(done)


def turned_gather(arrays, axis, dims):
    turned = [jnp.moveaxis(a, dim, 0) for a, dim in zip(arrays, dims)]
    both = jnp.concatenate([t.reshape(len(t), -1) for t in turned], axis=1)
    filled, at, done = (lax.all_gather(both, axis, axis=0, tiled=True), 0, [])
    for t, dim in zip(turned, dims):
        section = filled[:, at : at + t[0].size].reshape(-1, *t.shape[1:])
        done.append(jnp.moveaxis(section, 0, dim))
        at += t[0].size
    return tuple(done)


def correlate(padded, along_x, along_y):
    row_count = padded.shape[-2] - 2
    col_count = padded.shape[-1] - 2
    partial_x = None
    for offset in range(3):
        if along_x[offset] != 0.0:
            weighted = along_x[offset] * padded[..., offset : offset + row_count, :]
            partial_x = weighted if partial_x is None else partial_x + weighted
    running = None
    for offset in range(3):
        if along_y[offset] != 0.0:
            weighted = along_y[offset] * partial_x[..., offset : offset + col_count]
            running = weighted if running is None else running + weighted
    return running


def mirrored(padded, along_x, along_y):
    return correlate(padded, along_x[::-1], along_y[::-1])


def strains(padded):
    along_u, along_v, along_w = (padded[0], padded[1], padded[2])
    return jnp.stack(
        [
            correlate(along_u, BASIS_SLOPE, BASIS_VALUE),
            correlate(along_v, BASIS_VALUE, BASIS_SLOPE)
            + HOOP_CURVATURE * correlate(along_w, BASIS_VALUE, BASIS_VALUE),
            correlate(along_u, BASIS_VALUE, BASIS_SLOPE)
            + correlate(along_v, BASIS_SLOPE, BASIS_VALUE),
            -correlate(along_w, BASIS_CURVE, BASIS_VALUE),
            -correlate(along_w, BASIS_VALUE, BASIS_CURVE),
            -2.0 * correlate(along_w, BASIS_SLOPE, BASIS_SLOPE),
        ]
    )


def forces(spread):
    force_u = mirrored(spread[0], BASIS_SLOPE, BASIS_VALUE) + mirrored(
        spread[2], BASIS_VALUE, BASIS_SLOPE
    )
    force_v = mirrored(spread[1], BASIS_VALUE, BASIS_SLOPE) + mirrored(
        spread[2], BASIS_SLOPE, BASIS_VALUE
    )
    force_w = (
        HOOP_CURVATURE * mirrored(spread[1], BASIS_VALUE, BASIS_VALUE)
        - mirrored(spread[3], BASIS_CURVE, BASIS_VALUE)
        - mirrored(spread[4], BASIS_VALUE, BASIS_CURVE)
        - 2.0 * mirrored(spread[5], BASIS_SLOPE, BASIS_SLOPE)
    )
    return jnp.stack([force_u, force_v, force_w])


def apply_layup(stiffness_map, strain):
    running = stiffness_map[:, 0] * strain[0]
    for column in range(1, 6):
        running = running + stiffness_map[:, column] * strain[column]
    return running


def outer_product(left, right):
    return lax.dot_general(
        left, right, (((1,), (1,)), ((), ())), preferred_element_type=jnp.float32
    )


def forward_mlp(inputs, w_first, w_mid, w_last):
    hidden_layer = jnp.tanh(jnp.dot(w_first, inputs, preferred_element_type=jnp.float32)).astype(
        jnp.bfloat16
    )
    activations = [hidden_layer]
    for layer_index in range(w_mid.shape[0]):
        hidden_layer = jnp.tanh(
            jnp.dot(w_mid[layer_index], hidden_layer, preferred_element_type=jnp.float32)
        ).astype(jnp.bfloat16)
        activations.append(hidden_layer)
    return (jnp.dot(w_last, hidden_layer, preferred_element_type=jnp.float32), activations)


def backward_mlp(inputs, activations, upstream, w_mid, w_last):
    grad_last = outer_product(upstream, activations[-1])
    signal = jnp.dot(w_last.T, upstream, preferred_element_type=jnp.float32)
    derivative = (signal * (1.0 - jnp.square(activations[-1].astype(jnp.float32)))).astype(
        jnp.bfloat16
    )
    mid_grads = []
    for layer_index in range(w_mid.shape[0] - 1, -1, -1):
        mid_grads.append(outer_product(derivative, activations[layer_index]))
        signal = jnp.dot(w_mid[layer_index].T, derivative, preferred_element_type=jnp.float32)
        derivative = (
            signal * (1.0 - jnp.square(activations[layer_index].astype(jnp.float32)))
        ).astype(jnp.bfloat16)
    grad_first = outer_product(derivative, inputs)
    return (grad_first, jnp.stack(mid_grads[::-1]), grad_last)


def two_products(remainder, mapped):
    return (
        by_axis(jnp.sum(remainder * remainder), PATCH_SUB),
        by_axis(jnp.sum(remainder * mapped), PATCH_SUB),
    )


def careful(displacement, load, foundation, layup, layup_stiffness, w_first, w_mid, w_last):
    layup_count = layup_stiffness.shape[0]

    def coefficients(layup_ids):
        onehot = (
            layup_ids[None] == jnp.arange(layup_count, dtype=jnp.int32)[:, None, None]
        ).astype(jnp.float32)
        return jnp.einsum("lab,lxy->abxy", layup_stiffness, onehot, precision=lax.Precision.HIGHEST)

    stiffness_map = coefficients(layup)
    wide_ids = padded_2(layup, ((PATCH, 0), (SUB, 1)), 1)
    stiffness_wide = coefficients(wide_ids)

    def operate(search):
        padded = padded_2(search, ((PATCH, 1), (SUB, 2)), 2)
        return forces(apply_layup(stiffness_wide, strains(padded))) + foundation * search

    padded = padded_2(displacement, ((PATCH, 1), (SUB, 2)), 1)
    strain = strains(padded)
    inputs = strain.reshape(6, -1).astype(jnp.bfloat16)
    learned, activations = forward_mlp(inputs, w_first, w_mid, w_last)
    stress = apply_layup(stiffness_map, strain) + learned.reshape(strain.shape)
    spread = padded_2(stress, ((PATCH, 1), (SUB, 2)), 1)
    residual = forces(spread) + foundation * displacement - load
    adjoint = jnp.zeros_like(residual)
    remainder = residual
    mapped = operate(remainder)
    norm_now, curved = two_products(remainder, mapped)
    step_size = norm_now / curved
    direction, mapped_dir = (remainder, mapped)
    for step_index in range(ITERS):
        adjoint = adjoint + step_size * direction
        remainder = remainder - step_size * mapped_dir
        if step_index + 1 < ITERS:
            mapped = operate(remainder)
            norm_next, curved = two_products(remainder, mapped)
            beta_ratio = norm_next / norm_now
            step_size = norm_next / (curved - beta_ratio * norm_next / step_size)
            direction = remainder + beta_ratio * direction
            mapped_dir = mapped + beta_ratio * mapped_dir
            norm_now = norm_next
    cycle = padded_2(adjoint, ((PATCH, 1), (SUB, 2)), 1)
    upstream = strains(cycle).reshape(6, -1).astype(jnp.bfloat16)
    grad_first, grad_mid, grad_last = backward_mlp(inputs, activations, upstream, w_mid, w_last)
    shares = (
        sent_and_summed(grad_first, SUB, 0),
        sent_and_summed(grad_mid, SUB, 1),
        sent_and_summed(grad_last, SUB, 1),
    )
    crossed = packed_total((shares[0], shares[1], shares[2]), PATCH)
    totals = turned_gather((crossed[0], crossed[1], crossed[2]), SUB, (0, 1, 1))
    return (residual, adjoint, totals[0], totals[1], totals[2])


ROWS = 24
SEGS = 24
LANES = 128
OWN = 8
TILES = 16
STEP = 512
TRUST = 400.0
MESH = pl.DeviceIdType.MESH
PAIRS = [(a, b) for a in range(6) for b in range(a, 6)]
SPOT = {pair: k for k, pair in enumerate(PAIRS)}


def flat(ref):
    lead, mid, lanes = ref.shape
    return ref.reshape(lead * mid, lanes)


def column(ref, fields, field, row, segment):
    return flat(ref).at[pl.ds((row * fields + field) * SEGS + segment, 8, stride=fields * SEGS), :]


def lane_of():
    return lax.broadcasted_iota(jnp.int32, (SEGS, LANES), 1)


def after(field, lane):
    turned = pltpu.roll(field, LANES - 1, 1)
    return jnp.where(lane == LANES - 1, pltpu.roll(turned, SEGS - 1, 0), turned)


def before(field, lane):
    turned = pltpu.roll(field, 1, 1)
    return jnp.where(lane == 0, pltpu.roll(turned, 1, 0), turned)


def along_columns(read, y_ref, first, last):
    lane = lane_of()

    def body(e, carry):
        u, v, w = read(e)
        at = e * 7
        for k, field in enumerate((u, v, w)):
            ahead, behind = after(field, lane), before(field, lane)
            both = ahead + behind
            y_ref[at + 2 * k] = 0.75 * field + 0.125 * both
            y_ref[at + 2 * k + 1] = 0.5 * (ahead - behind)
            if k == 2:
                y_ref[at + 6] = both - 2.0 * field
        return carry

    lax.fori_loop(first, last, body, 0, unroll=2)


def strains_at(y_ref, e):
    at = e * 7

    def three(k):
        return y_ref[at - 7 + k], y_ref[at + k], y_ref[at + 7 + k]

    def value(k):
        m, c, p = three(k)
        return 0.75 * c + 0.125 * (p + m)

    def slope(k):
        return 0.5 * (y_ref[at + 7 + k] - y_ref[at - 7 + k])

    m, c, p = three(4)
    pair = p + m
    return [
        slope(0),
        value(3) + HOOP_CURVATURE * (0.75 * c + 0.125 * pair),
        value(1) + slope(2),
        2.0 * c - pair,
        -value(6),
        y_ref[at - 7 + 5] - y_ref[at + 7 + 5],
    ]


def laminate(c_ref, e, strain):
    at = e * 21
    total = [None] * 6
    for (a, b), k in SPOT.items():
        c = c_ref[at + k]
        term = c * strain[b]
        total[a] = term if total[a] is None else total[a] + term
        if a != b:
            term = c * strain[a]
            total[b] = term if total[b] is None else total[b] + term
    return total


def forces_at(s_ref, e, lane):
    at = e * 6

    def three(k):
        return s_ref[at - 6 + k], s_ref[at + k], s_ref[at + 6 + k]

    def value(k):
        m, c, p = three(k)
        return 0.75 * c + 0.125 * (p + m)

    def slope(k):
        return 0.5 * (s_ref[at - 6 + k] - s_ref[at + 6 + k])

    def spread(here, behind, ahead):
        return here + before(behind, lane) + after(ahead, lane)

    a, b = slope(0), value(2)
    force_u = spread(0.75 * a, 0.125 * a + 0.5 * b, 0.125 * a - 0.5 * b)
    a, b = slope(2), value(1)
    force_v = spread(0.75 * a, 0.125 * a + 0.5 * b, 0.125 * a - 0.5 * b)
    m, c, p = three(3)
    a = HOOP_CURVATURE * b - ((m + p) - 2.0 * c)
    d = value(4)
    half = slope(5)
    base = 0.125 * a - d
    force_w = spread(0.75 * a + 2.0 * d, base - half, base + half)
    return force_u, force_v, force_w


def fused(
    disp_in, load_in, found_in, lay_in, stiff, w1t, wm, wl,
    res_o, adj_o, gf_o, gm_o, gl_o, trust_o,
    disp, load, found, lay, in_s, dsp, aux, ids, lod, edge_a, edge_c, got_a, got_c, y_ref, s_ref, c_ref, x_ref, l_ref, u_ref, h_ref,
    v0, v1, v2, v3, wmt, acc_m, acc_s,
    d_out, d_in, d_mid, d_in2, e_out, e_in, e_mid, e_in2, e_end, e_in3,
    g_out, g_in, g_mid, g_in2, g_end, g_in3,
    a_s, a_r, c_s, c_r, d1_s, d1_r, d2_s, d2_r, e1_s, e1_r, e2_s, e2_r, e3_s, e3_r,
    g1_s, g1_r, g2_s, g2_r, g3_s, g3_r,
):
    me_p, me_s = lax.axis_index("patch"), lax.axis_index("sub")
    count_p, count_s = lax.axis_size("patch"), lax.axis_size("sub")

    def place(dp, ds):
        return {"patch": lax.rem(me_p + dp, count_p), "sub": lax.rem(me_s + ds, count_s)}

    up, down = count_p - 1, 1
    left, right = count_s - 1, 1
    greeted = [(0, k) for k in range(1, count_s)] + [(k, 0) for k in range(1, count_p)]
    greeted += [(a, b) for a in (up, down) for b in (left, right)]
    barrier = pltpu.get_barrier_semaphore()
    for dp, ds in greeted:
        pl.semaphore_signal(barrier, inc=1, device_id=place(dp, ds), device_id_type=MESH)

    arriving = [
        pltpu.make_async_copy(source, held, in_s.at[k])
        for k, (source, held) in enumerate(((disp_in, disp), (lay_in, lay), (found_in, found), (load_in, load)))
    ]
    for copy in arriving:
        copy.start()
    for copy in arriving[:3]:
        copy.wait()

    for t in range(TILES):
        cut = pl.ds(t * LANES, LANES)
        for f in range(3):
            column(dsp, 3, f, OWN, 8 + t)[...] = disp[f, :, cut]
        column(ids, 1, 0, OWN, 8 + t)[...] = lay[:, cut].astype(jnp.float32)
    ends = ((0, pl.ds(0, LANES)), (1, pl.ds((TILES - 1) * LANES, LANES)))
    for side, cut in ends:
        for f in range(3):
            edge_a[side, f] = disp[f, :, cut]
            edge_a[side, 4 + f] = found[f, :, cut]
        edge_a[side, 3] = lay[:, cut].astype(jnp.float32)

    pl.semaphore_wait(barrier, len(greeted))

    def send(src, dst, sent, received, to):
        return pltpu.make_async_remote_copy(
            src_ref=src, dst_ref=dst, send_sem=sent, recv_sem=received, device_id=to, device_id_type=MESH
        )

    def rows_to(ref, fields, near, far, sent, received, first):
        own, n = pl.ds(OWN, TILES), (far - near) * fields
        below = send(
            ref.at[pl.ds((16 - far) * fields, n), own, :],
            ref.at[pl.ds((8 - far) * fields, n), own, :],
            sent.at[first], received.at[first], place(down, 0),
        )
        above = send(
            ref.at[pl.ds((8 + near) * fields, n), own, :],
            ref.at[pl.ds((16 + near) * fields, n), own, :],
            sent.at[first + 1], received.at[first + 1], place(up, 0),
        )
        return [below, above]

    heading = ((0, right, 1), (0, left, 0), (down, right, 1), (down, left, 0), (up, right, 1), (up, left, 0))

    def edges_to(edge, got, fields, sent, received, first):
        return [
            send(edge.at[side, fields], got.at[k, fields], sent.at[first + k], received.at[first + k], place(dp, ds))
            for k, (dp, ds, side) in reversed(list(enumerate(heading)))
        ]

    def start(copies):
        for copy in copies:
            copy.start()

    landing = ((7, 8), (0, 8), (7, 0), (0, 0), (7, 16), (0, 16))

    first_a = (
        edges_to(edge_a, got_a, pl.ds(0, 4), a_s, a_r, 2)
        + rows_to(dsp, 3, 0, 2, a_s, a_r, 0)
        + rows_to(ids, 1, 0, 1, a_s, a_r, 8)
    )
    start(first_a)
    arriving[3].wait()
    for t in range(TILES):
        cut = pl.ds(t * LANES, LANES)
        for f in range(3):
            column(aux, 3, f, OWN, 8 + t)[...] = found[f, :, cut]
            column(lod, 3, f, 0, 8 + t)[...] = load[f, :, cut]
    for k in range(3):
        wmt[k] = wm[k].T
    w1 = w1t[...].T
    wlt = wl[...].T

    def choose_row(e, carry):
        kind = ids[e].astype(jnp.int32)
        low, middle, high = (kind & 1) == 1, (kind & 2) == 2, (kind & 4) == 4
        for k, (a, b) in enumerate(PAIRS):
            p = [jnp.where(low, stiff[a, 2 * q + 1, b], stiff[a, 2 * q, b]) for q in range(4)]
            c_ref[e * 21 + k] = jnp.where(
                high, jnp.where(middle, p[3], p[2]), jnp.where(middle, p[1], p[0])
            )
        return carry

    for copy in first_a:
        copy.wait()
    second_a = (
        rows_to(aux, 3, 0, 5, a_s, a_r, 10)
        + rows_to(ids, 1, 1, 6, a_s, a_r, 12)
        + edges_to(edge_a, got_a, pl.ds(4, 3), a_s, a_r, 14)
    )
    start(second_a)
    for k, (segment, row) in enumerate(landing):
        for f in range(3):
            column(dsp, 3, f, row, segment)[...] = got_a[k, f]
        column(ids, 1, 0, row, segment)[...] = got_a[k, 3]

    lane = lane_of()
    along_columns(lambda e: [dsp[e * 3 + f] for f in range(3)], y_ref, 6, 18)

    def strain_row(r, carry):
        e = r + 7
        strain = strains_at(y_ref, e)
        for k in range(6):
            s_ref[e * 6 + k] = strain[k]
            flat(x_ref)[pl.ds(r * (SEGS * 8) + k, SEGS, stride=8), :] = strain[k]
        return carry

    lax.fori_loop(0, 10, strain_row, 0, unroll=2)
    tile_lane = lax.broadcasted_iota(jnp.int32, (8, LANES), 1)
    beside = 10 * SEGS
    packed = jnp.zeros((8, LANES), jnp.float32)
    for r in range(10):
        ends_of = jnp.where(tile_lane < 64, x_ref[r * SEGS], x_ref[r * SEGS + 7])
        turned = pltpu.roll(ends_of, 2 * r + 1, 1)
        packed = jnp.where((tile_lane == 2 * r) | (tile_lane == 2 * r + 1), turned, packed)
    x_ref[beside] = packed

    def operand(ref, at, width):
        tiles = [ref[at + q] for q in range(width // LANES)]
        return jnp.concatenate(tiles, axis=1)[:6].astype(jnp.bfloat16)

    def learn(parts):
        for at, slot, first, width in parts:
            h_ref[slot, :, pl.ds(first, width)] = jnp.tanh(
                jnp.dot(w1, operand(x_ref, at, width), preferred_element_type=jnp.float32)
            ).astype(jnp.bfloat16)
        for k in range(3):
            for at, slot, first, width in parts:
                cut = pl.ds(first, width)
                h_ref[slot + k + 1, :, cut] = jnp.tanh(
                    jnp.dot(wm[k], h_ref[slot + k, :, cut], preferred_element_type=jnp.float32)
                ).astype(jnp.bfloat16)
        for at, slot, first, width in parts:
            out = jnp.dot(wl[...], h_ref[slot + 3, :, pl.ds(first, width)], preferred_element_type=jnp.float32)
            for q in range(width // LANES):
                l_ref[at + q, 0:6, :] = out[:, q * LANES : (q + 1) * LANES]

    def row_parts(r, slot):
        return [
            (r * SEGS + 8 + c * (STEP // LANES), slot, c * STEP, STEP) for c in range(2048 // STEP)
        ]

    def stress_row(r):
        e = r + 7
        choose_row(e, 0)
        stress = laminate(c_ref, e, [s_ref[e * 6 + k] for k in range(6)])
        for k in range(6):
            s_ref[e * 6 + k] = stress[k] + flat(l_ref)[pl.ds(r * (SEGS * 8) + k, SEGS, stride=8), :]

    def residual_row(e):
        force = forces_at(s_ref, e, lane)
        for f in range(3):
            v0[e * 3 + f] = force[f] + aux[e * 3 + f] * dsp[e * 3 + f] - lod[(e - 8) * 3 + f]

    def residual_to(e):
        own, row = pl.ds(OWN, TILES), v0.at[pl.ds(e * 3, 3), pl.ds(OWN, TILES), :]
        return [
            send(row, v0.at[pl.ds((e - 8) * 3, 3), own, :], c_s.at[e - 2], c_r.at[e - 2], place(down, 0)),
            send(row, v0.at[pl.ds((e + 8) * 3, 3), own, :], c_s.at[e + 6], c_r.at[e + 6], place(up, 0)),
        ]

    learn([(beside, 32, 0, LANES)] + row_parts(0, 36))
    for r in range(10):
        turned = pltpu.roll(l_ref[beside], LANES - 1 - 2 * r, 1)
        l_ref[r * SEGS] = turned
        l_ref[r * SEGS + 7] = turned
    for r in (1, 2):
        stress_row(r - 1)
        learn(row_parts(r, (r - 1) * 4))

    def pipelined_row(r, carry):
        @pl.when(r > 3)
        def _():
            start(residual_to(r + 4))

        stress_row(r - 1)
        residual_row(r + 5)
        learn(row_parts(r, (r - 1) * 4))
        return carry

    lax.fori_loop(3, 10, pipelined_row, 0)
    start(residual_to(14))
    stress_row(9)
    residual_row(15)
    start(residual_to(15))
    for side, t in ((0, 0), (1, TILES - 1)):
        for f in range(3):
            edge_c[side, f] = column(v0, 3, f, OWN, 8 + t)[...]
    moves_c = edges_to(edge_c, got_c, pl.ds(0, 3), c_s, c_r, 0)
    start(moves_c)
    for copy in second_a:
        copy.wait()
    for k, (segment, row) in enumerate(landing):
        for f in range(3):
            column(aux, 3, f, row, segment)[...] = got_a[k, 4 + f]
    lax.fori_loop(2, 7, choose_row, 0)
    lax.fori_loop(17, 22, choose_row, 0)
    for t in range(TILES):
        for f in range(3):
            res_o[f, :, pl.ds(t * LANES, LANES)] = column(v0, 3, f, OWN, 8 + t)[...]
    for copy in moves_c:
        copy.wait()
    for e in range(8, 16):
        for copy in residual_to(e):
            copy.wait()
    for k, (segment, row) in enumerate(landing):
        for f in range(3):
            column(v0, 3, f, row, segment)[...] = got_c[k, f]

    def mean(k):
        total = stiff[k, 0, k]
        for q in range(1, 8):
            total = total + stiff[k, q, k]
        return total * 0.125

    half = 1.0 + 8.0 * jnp.maximum(mean(3), mean(4))
    center = jnp.full((1, LANES), half, jnp.float32)
    inverse = 1.0 / center

    def apply_stiffness(v, older, out, first, last):
        along_columns(lambda e: [v[e * 3 + f] for f in range(3)], y_ref, first - 2, last + 2)

        def body(e, carry):
            stress = laminate(c_ref, e, strains_at(y_ref, e))
            for k in range(6):
                s_ref[e * 6 + k] = stress[k]
            return carry

        lax.fori_loop(first - 1, last + 1, body, 0, unroll=2)

        def finish(e, carry):
            force = forces_at(s_ref, e, lane)
            for f in range(3):
                here = v[e * 3 + f]
                image = force[f] + aux[e * 3 + f] * here
                if older is None:
                    out[e * 3 + f] = inverse * image - here
                else:
                    out[e * 3 + f] = (2.0 * inverse) * image - 2.0 * here - older[e * 3 + f]
            return carry

        lax.fori_loop(first, last, finish, 0, unroll=2)

    apply_stiffness(v0, None, v1, 3, 21)
    apply_stiffness(v1, v0, v2, 5, 19)
    apply_stiffness(v2, v1, v3, 7, 17)
    along_columns(lambda e: [v3[e * 3 + f] for f in range(3)], y_ref, 7, 17)

    def folded(field):
        return field[8:16] + field[16:24]

    def sums_row(e, totals):
        strain = strains_at(y_ref, e)
        stress = laminate(c_ref, e, strain)
        energy = strain[0] * stress[0]
        for k in range(1, 6):
            energy = energy + strain[k] * stress[k]
        totals = list(totals)
        for f in range(3):
            a, b, c, d = v0[e * 3 + f], v1[e * 3 + f], v2[e * 3 + f], v3[e * 3 + f]
            energy = energy + aux[e * 3 + f] * (d * d)
            for k, product in enumerate((a * a, a * b, b * b, b * c, c * c, c * d, d * d)):
                totals[k] = totals[k] + folded(product)
        totals[7] = totals[7] + folded(energy)
        return tuple(totals)

    totals = lax.fori_loop(8, 16, sums_row, tuple(jnp.zeros((8, LANES), jnp.float32) for _ in range(8)), unroll=2)
    d_out[...] = jnp.concatenate([jnp.sum(t, axis=0, keepdims=True) for t in totals], axis=0)

    def farthest_first(count):
        return sorted(range(1, count), key=lambda k: (-min(k, count - k) - 2 * (k % 2), k))

    def shared(source, slots, sent, received, count, mine, spot, piece=None):
        copies = []
        for k in farthest_first(count):
            src = source if piece is None else source.at[lax.rem(mine + k, count)]
            copies.append(send(src, slots.at[mine], sent.at[k], received.at[mine], spot(k)))
        start(copies)
        own = source if piece is None else source.at[mine]
        slots[mine] = own[...]

        def finish():
            for k in range(1, count):
                other = lax.rem(mine + k, count)
                src = source if piece is None else source.at[other]
                send(src, slots.at[other], sent.at[k], received.at[other], spot(k)).wait()

        return finish

    def summed(slots, count):
        total = slots[0]
        for k in range(1, count):
            total = total + slots[k]
        return total

    by_sub, by_patch = (lambda k: place(0, k)), (lambda k: place(k, 0))
    shared(d_out, d_in, d1_s, d1_r, count_s, me_s, by_sub)()
    d_mid[...] = summed(d_in, count_s)
    shared(d_mid, d_in2, d2_s, d2_r, count_p, me_p, by_patch)()
    everyone = jnp.sum(summed(d_in2, count_p), axis=1, keepdims=True)
    n = [jnp.broadcast_to(everyone[k : k + 1], (1, LANES)) for k in range(8)]
    n34 = (2.0 * inverse) * n[7] - 2.0 * n[6] - n[5]
    m = [n[0], n[1]]
    for k in (2, 3, 4, 5, 6):
        m.append(2.0 * n[k] - m[k % 2])
    m.append(2.0 * n34 - m[1])

    def gram(i, j):
        return 0.5 * (m[i + j] + m[abs(i - j)])

    def form(x, y):
        total, size = None, None
        for i, a in enumerate(x):
            for j, b in enumerate(y):
                term = a * b * gram(i, j)
                total = term if total is None else total + term
                size = jnp.abs(term) if size is None else size + jnp.abs(term)
        return total, size / total

    def image_of(x):
        zero = jnp.zeros((1, LANES), jnp.float32)
        out = [center * a for a in x] + [zero]
        for j, a in enumerate(x):
            if j == 0:
                out[1] = out[1] + center * a
            else:
                out[j + 1] = out[j + 1] + (0.5 * center) * a
                out[j - 1] = out[j - 1] + (0.5 * center) * a
        return out

    one = jnp.ones((1, LANES), jnp.float32)
    zero = jnp.zeros((1, LANES), jnp.float32)
    rest, way, found_y, norm = [one], [one], [zero] * 4, m[0]
    worst = one
    for step in range(ITERS):
        image = image_of(way)
        curved, spread = form(way, image)
        worst = jnp.where(spread <= TRUST, worst, 2.0 * TRUST * one)
        alpha = norm / curved
        found_y = [found_y[k] + alpha * way[k] if k < len(way) else found_y[k] for k in range(4)]
        if step + 1 < ITERS:
            rest = [(rest[k] if k < len(rest) else zero) - alpha * image[k] for k in range(len(image))]
            fresh, spread = form(rest, rest)
            worst = jnp.where(spread <= TRUST, worst, 2.0 * TRUST * one)
            beta = fresh / norm
            way = [rest[k] + (beta * way[k] if k < len(way) else zero) for k in range(len(rest))]
            norm = fresh
    trust_o[0, 0] = worst[0, 0]

    def adjoint_row(e, carry):
        for f in range(3):
            at = e * 3 + f
            v0[at] = found_y[0] * v0[at] + found_y[1] * v1[at] + found_y[2] * v2[at] + found_y[3] * v3[at]
        return carry

    lax.fori_loop(7, 17, adjoint_row, 0, unroll=2)
    for t in range(TILES):
        for f in range(3):
            adj_o[f, :, pl.ds(t * LANES, LANES)] = column(v0, 3, f, OWN, 8 + t)[...]
    along_columns(lambda e: [v0[e * 3 + f] for f in range(3)], y_ref, 7, 17)

    def upstream_row(e, carry):
        strain = strains_at(y_ref, e)
        for k in range(6):
            flat(u_ref)[pl.ds((e - 8) * (SEGS * 8) + k, SEGS, stride=8), :] = strain[k]
        return carry

    lax.fori_loop(8, 16, upstream_row, 0, unroll=2)

    acc_m[...] = jnp.zeros_like(acc_m)
    acc_s[...] = jnp.zeros_like(acc_s)

    def derive(weights, signal_of, slot):
        for c in range(2048 // STEP):
            cut = pl.ds(c * STEP, STEP)
            h = h_ref[slot, :, cut].astype(jnp.float32)
            signal = jnp.dot(weights, signal_of(c, cut), preferred_element_type=jnp.float32)
            h_ref[slot, :, cut] = (signal * (1.0 - jnp.square(h))).astype(jnp.bfloat16)

    def back_last(r, carry):
        slot = r * 4 + 3
        u = operand(u_ref, r * SEGS + 8, 2048)
        acc_s[0:6] += outer_product(u, h_ref[slot])
        derive(wlt, lambda c, cut: u[:, c * STEP : (c + 1) * STEP], slot)
        return carry

    def back_mid(k):
        def body(r, carry):
            slot = r * 4 + k
            acc_m[k] += outer_product(h_ref[slot + 1], h_ref[slot])
            derive(wmt[k], lambda c, cut: h_ref[slot + 1, :, cut], slot)
            return carry

        lax.fori_loop(0, 8, body, 0)

    def back_first(r, carry):
        acc_s[8:14] += outer_product(operand(x_ref, (r + 1) * SEGS + 8, 2048), h_ref[r * 4])
        return carry

    lax.fori_loop(0, 8, back_last, 0)
    back_mid(2)
    back_mid(1)
    for k in range(16):
        e_out[k, 0:8, :] = acc_m[1, 8 * k : 8 * k + 8]
        e_out[k, 8:16, :] = acc_m[2, 8 * k : 8 * k + 8]
    finish_e1 = shared(e_out, e_in, e1_s, e1_r, count_s, me_s, by_sub, piece=True)
    back_mid(0)
    lax.fori_loop(0, 8, back_first, 0, unroll=2)
    for k in range(16):
        g_out[k, 0:8, :] = acc_m[0, 8 * k : 8 * k + 8]
        g_out[k, 8:9, :] = acc_s[k : k + 1]
    finish_g1 = shared(g_out, g_in, g1_s, g1_r, count_s, me_s, by_sub, piece=True)
    finish_e1()
    e_mid[...] = summed(e_in, count_s)
    finish_e2 = shared(e_mid, e_in2, e2_s, e2_r, count_p, me_p, by_patch)
    finish_g1()
    g_mid[...] = summed(g_in, count_s)
    finish_g2 = shared(g_mid, g_in2, g2_s, g2_r, count_p, me_p, by_patch)
    finish_e2()
    e_end[...] = summed(e_in2, count_p)
    finish_e3 = shared(e_end, e_in3, e3_s, e3_r, count_s, me_s, by_sub)
    finish_g2()
    g_end[...] = summed(g_in2, count_p)
    finish_g3 = shared(g_end, g_in3, g3_s, g3_r, count_s, me_s, by_sub)
    finish_e3()
    for k in range(16):
        gm_o[1, 8 * k : 8 * k + 8] = e_in3[k, 0:8, :]
        gm_o[2, 8 * k : 8 * k + 8] = e_in3[k, 8:16, :]
    finish_g3()
    for k in range(16):
        gm_o[0, 8 * k : 8 * k + 8] = g_in3[k, 0:8, :]
    for k in range(6):
        gl_o[k : k + 1] = g_in3[k, 8:9, :]
        gf_o[k : k + 1] = g_in3[8 + k, 8:9, :]


def per_device(displacement, load, foundation, layup, layup_stiffness, w_first, w_mid, w_last):
    vmem = pl.BlockSpec(memory_space=pltpu.VMEM)
    smem = pl.BlockSpec(memory_space=pltpu.SMEM)
    f32, bf16 = jnp.float32, jnp.bfloat16

    def rows(fields, count=ROWS):
        return pltpu.VMEM((count * fields, SEGS, LANES), f32)

    dma = pltpu.SemaphoreType.DMA
    out = pl.pallas_call(
        fused,
        out_shape=[
            jax.ShapeDtypeStruct(displacement.shape, f32),
            jax.ShapeDtypeStruct(displacement.shape, f32),
            jax.ShapeDtypeStruct((6, 128), f32),
            jax.ShapeDtypeStruct((3, 128, 128), f32),
            jax.ShapeDtypeStruct((6, 128), f32),
            jax.ShapeDtypeStruct((1, 1), f32),
        ],
        in_specs=[pl.BlockSpec(memory_space=pl.ANY)] * 4 + [smem] + [vmem] * 3,
        out_specs=[vmem] * 5 + [smem],
        scratch_shapes=[
            pltpu.VMEM(displacement.shape, f32), pltpu.VMEM(displacement.shape, f32),
            pltpu.VMEM(displacement.shape, f32), pltpu.VMEM(layup.shape, jnp.int32), dma((4,)),
            rows(3), rows(3), rows(1), rows(3, 8),
            pltpu.VMEM((2, 7, 8, LANES), f32), pltpu.VMEM((2, 3, 8, LANES), f32),
            pltpu.VMEM((6, 7, 8, LANES), f32), pltpu.VMEM((6, 3, 8, LANES), f32),
            rows(7), rows(6), rows(21),
            pltpu.VMEM((11 * SEGS, 8, LANES), f32),
            pltpu.VMEM((11 * SEGS, 8, LANES), f32),
            pltpu.VMEM((8 * SEGS, 8, LANES), f32),
            pltpu.VMEM((10 * 4, 128, 2048), bf16),
            rows(3), rows(3), rows(3), rows(3),
            pltpu.VMEM((3, 128, 128), bf16),
            pltpu.VMEM((3, 128, 128), f32), pltpu.VMEM((16, 128), f32),
            pltpu.VMEM((8, LANES), f32), pltpu.VMEM((16, 8, LANES), f32),
            pltpu.VMEM((8, LANES), f32), pltpu.VMEM((16, 8, LANES), f32),
        ] + [
            pltpu.VMEM(shape, f32)
            for n in (16, 9)
            for shape in [(16, n, LANES), (16, n, LANES), (n, LANES)] + [(16, n, LANES), (n, LANES), (16, n, LANES)]
        ] + [
            dma((20,)), dma((20,)), dma((22,)), dma((22,)),
        ] + [dma((16,)) for _ in range(16)],
        compiler_params=pltpu.CompilerParams(
            collective_id=0, has_side_effects=True, vmem_limit_bytes=46 << 20
        ),
        name="adjoint_step",
    )(
        displacement, load, foundation, layup, layup_stiffness.transpose(1, 0, 2), w_first.T, w_mid, w_last
    )
    fast, trust = (out[0], out[1], out[2].T, out[3], out[4]), out[5][0, 0]
    operands = (displacement, load, foundation, layup, layup_stiffness, w_first, w_mid, w_last)
    return lax.cond(trust <= TRUST, lambda: fast, lambda: careful(*operands))


def solution(mesh):
    return jax.shard_map(
        per_device,
        mesh=mesh,
        in_specs=(
            P(None, "patch", "sub"),
            P(None, "patch", "sub"),
            P(None, "patch", "sub"),
            P("patch", "sub"),
            P(),
            P(),
            P(),
            P(),
        ),
        out_specs=(P(None, "patch", "sub"), P(None, "patch", "sub"), P(), P(), P()),
        check_vma=False,
    )
```

```python
import functools

import jax
import jax.numpy as jnp
from jax import lax
from jax.experimental import pallas as pl
from jax.experimental.pallas import tpu as pltpu
from jax.sharding import PartitionSpec as P

ITERS = 4
PATCH_SUB = ("patch", "sub")
PATCH = "patch"
SUB = "sub"


BASIS_VALUE = (0.125, 0.75, 0.125)
BASIS_SLOPE = (-0.5, 0.0, 0.5)
BASIS_CURVE = (1.0, -2.0, 1.0)
HOOP_CURVATURE = 0.25


def by_axis(value, axes):
    return lax.psum(value, axes)


def padded_2(cells, sides, width):
    for axis, dim in sides:
        count = lax.axis_size(axis)
        head = lax.slice_in_dim(cells, 0, width, axis=dim)
        tail = lax.slice_in_dim(cells, cells.shape[dim] - width, cells.shape[dim], axis=dim)
        cells = jnp.concatenate(
            [
                lax.ppermute(tail, axis, [(i, (i + 1) % count) for i in range(count)]),
                cells,
                lax.ppermute(head, axis, [((i + 1) % count, i) for i in range(count)]),
            ],
            axis=dim,
        )
    return cells


def split_up(value, dim, size):
    lengths = value.shape
    pieces = value.reshape(*lengths[:dim], size, lengths[dim] // size, *lengths[dim + 1 :])
    return jnp.moveaxis(pieces, dim, 0)


def sent_and_summed(value, axis, dim):
    size = lax.axis_size(axis)
    pieces = lax.all_to_all(split_up(value, dim, size), axis, 0, 0, tiled=True)
    return jnp.sum(pieces, axis=0)


def sent_to_all(value, axis):
    size = lax.axis_size(axis)
    return lax.all_to_all(
        jnp.broadcast_to(value[None], (size, *value.shape)), axis, 0, 0, tiled=True
    )


def of_everyone(value, axis):
    return sent_to_all(value, axis).sum(axis=0)


def packed_total(arrays, axis):
    vector, at, done = (jnp.concatenate([a.reshape(-1) for a in arrays]), 0, [])
    subtotal = of_everyone(vector, axis)
    for a in arrays:
        done.append(subtotal[at : at + a.size].reshape(a.shape))
        at += a.size
    return tuple(done)


def turned_gather(arrays, axis, dims):
    turned = [jnp.moveaxis(a, dim, 0) for a, dim in zip(arrays, dims)]
    both = jnp.concatenate([t.reshape(len(t), -1) for t in turned], axis=1)
    filled, at, done = (lax.all_gather(both, axis, axis=0, tiled=True), 0, [])
    for t, dim in zip(turned, dims):
        section = filled[:, at : at + t[0].size].reshape(-1, *t.shape[1:])
        done.append(jnp.moveaxis(section, 0, dim))
        at += t[0].size
    return tuple(done)


def correlate(padded, along_x, along_y):
    row_count = padded.shape[-2] - 2
    col_count = padded.shape[-1] - 2
    partial_x = None
    for offset in range(3):
        if along_x[offset] != 0.0:
            weighted = along_x[offset] * padded[..., offset : offset + row_count, :]
            partial_x = weighted if partial_x is None else partial_x + weighted
    running = None
    for offset in range(3):
        if along_y[offset] != 0.0:
            weighted = along_y[offset] * partial_x[..., offset : offset + col_count]
            running = weighted if running is None else running + weighted
    return running


def mirrored(padded, along_x, along_y):
    return correlate(padded, along_x[::-1], along_y[::-1])


def strains(padded):
    along_u, along_v, along_w = (padded[0], padded[1], padded[2])
    return jnp.stack(
        [
            correlate(along_u, BASIS_SLOPE, BASIS_VALUE),
            correlate(along_v, BASIS_VALUE, BASIS_SLOPE)
            + HOOP_CURVATURE * correlate(along_w, BASIS_VALUE, BASIS_VALUE),
            correlate(along_u, BASIS_VALUE, BASIS_SLOPE)
            + correlate(along_v, BASIS_SLOPE, BASIS_VALUE),
            -correlate(along_w, BASIS_CURVE, BASIS_VALUE),
            -correlate(along_w, BASIS_VALUE, BASIS_CURVE),
            -2.0 * correlate(along_w, BASIS_SLOPE, BASIS_SLOPE),
        ]
    )


def forces(spread):
    force_u = mirrored(spread[0], BASIS_SLOPE, BASIS_VALUE) + mirrored(
        spread[2], BASIS_VALUE, BASIS_SLOPE
    )
    force_v = mirrored(spread[1], BASIS_VALUE, BASIS_SLOPE) + mirrored(
        spread[2], BASIS_SLOPE, BASIS_VALUE
    )
    force_w = (
        HOOP_CURVATURE * mirrored(spread[1], BASIS_VALUE, BASIS_VALUE)
        - mirrored(spread[3], BASIS_CURVE, BASIS_VALUE)
        - mirrored(spread[4], BASIS_VALUE, BASIS_CURVE)
        - 2.0 * mirrored(spread[5], BASIS_SLOPE, BASIS_SLOPE)
    )
    return jnp.stack([force_u, force_v, force_w])


def apply_layup(stiffness_map, strain):
    running = stiffness_map[:, 0] * strain[0]
    for column in range(1, 6):
        running = running + stiffness_map[:, column] * strain[column]
    return running


def outer_product(left, right):
    return lax.dot_general(
        left, right, (((1,), (1,)), ((), ())), preferred_element_type=jnp.float32
    )


def forward_mlp(inputs, w_first, w_mid, w_last):
    hidden_layer = jnp.tanh(jnp.dot(w_first, inputs, preferred_element_type=jnp.float32)).astype(
        jnp.bfloat16
    )
    activations = [hidden_layer]
    for layer_index in range(w_mid.shape[0]):
        hidden_layer = jnp.tanh(
            jnp.dot(w_mid[layer_index], hidden_layer, preferred_element_type=jnp.float32)
        ).astype(jnp.bfloat16)
        activations.append(hidden_layer)
    return (jnp.dot(w_last, hidden_layer, preferred_element_type=jnp.float32), activations)


def backward_mlp(inputs, activations, upstream, w_mid, w_last):
    grad_last = outer_product(upstream, activations[-1])
    signal = jnp.dot(w_last.T, upstream, preferred_element_type=jnp.float32)
    derivative = (signal * (1.0 - jnp.square(activations[-1].astype(jnp.float32)))).astype(
        jnp.bfloat16
    )
    mid_grads = []
    for layer_index in range(w_mid.shape[0] - 1, -1, -1):
        mid_grads.append(outer_product(derivative, activations[layer_index]))
        signal = jnp.dot(w_mid[layer_index].T, derivative, preferred_element_type=jnp.float32)
        derivative = (
            signal * (1.0 - jnp.square(activations[layer_index].astype(jnp.float32)))
        ).astype(jnp.bfloat16)
    grad_first = outer_product(derivative, inputs)
    return (grad_first, jnp.stack(mid_grads[::-1]), grad_last)


def two_products(remainder, mapped):
    return (
        by_axis(jnp.sum(remainder * remainder), PATCH_SUB),
        by_axis(jnp.sum(remainder * mapped), PATCH_SUB),
    )


def careful(displacement, load, foundation, layup, layup_stiffness, w_first, w_mid, w_last):
    layup_count = layup_stiffness.shape[0]

    def coefficients(layup_ids):
        onehot = (
            layup_ids[None] == jnp.arange(layup_count, dtype=jnp.int32)[:, None, None]
        ).astype(jnp.float32)
        return jnp.einsum("lab,lxy->abxy", layup_stiffness, onehot, precision=lax.Precision.HIGHEST)

    stiffness_map = coefficients(layup)
    wide_ids = padded_2(layup, ((PATCH, 0), (SUB, 1)), 1)
    stiffness_wide = coefficients(wide_ids)

    def operate(search):
        padded = padded_2(search, ((PATCH, 1), (SUB, 2)), 2)
        return forces(apply_layup(stiffness_wide, strains(padded))) + foundation * search

    padded = padded_2(displacement, ((PATCH, 1), (SUB, 2)), 1)
    strain = strains(padded)
    inputs = strain.reshape(6, -1).astype(jnp.bfloat16)
    learned, activations = forward_mlp(inputs, w_first, w_mid, w_last)
    stress = apply_layup(stiffness_map, strain) + learned.reshape(strain.shape)
    spread = padded_2(stress, ((PATCH, 1), (SUB, 2)), 1)
    residual = forces(spread) + foundation * displacement - load
    adjoint = jnp.zeros_like(residual)
    remainder = residual
    mapped = operate(remainder)
    norm_now, curved = two_products(remainder, mapped)
    step_size = norm_now / curved
    direction, mapped_dir = (remainder, mapped)
    for step_index in range(ITERS):
        adjoint = adjoint + step_size * direction
        remainder = remainder - step_size * mapped_dir
        if step_index + 1 < ITERS:
            mapped = operate(remainder)
            norm_next, curved = two_products(remainder, mapped)
            beta_ratio = norm_next / norm_now
            step_size = norm_next / (curved - beta_ratio * norm_next / step_size)
            direction = remainder + beta_ratio * direction
            mapped_dir = mapped + beta_ratio * mapped_dir
            norm_now = norm_next
    cycle = padded_2(adjoint, ((PATCH, 1), (SUB, 2)), 1)
    upstream = strains(cycle).reshape(6, -1).astype(jnp.bfloat16)
    grad_first, grad_mid, grad_last = backward_mlp(inputs, activations, upstream, w_mid, w_last)
    shares = (
        sent_and_summed(grad_first, SUB, 0),
        sent_and_summed(grad_mid, SUB, 1),
        sent_and_summed(grad_last, SUB, 1),
    )
    crossed = packed_total((shares[0], shares[1], shares[2]), PATCH)
    totals = turned_gather((crossed[0], crossed[1], crossed[2]), SUB, (0, 1, 1))
    return (residual, adjoint, totals[0], totals[1], totals[2])


ROWS = 24
SEGS = 24
LANES = 128
OWN = 8
TILES = 16
STEP = 512
TRUST = 400.0
MESH = pl.DeviceIdType.MESH
PAIRS = [(a, b) for a in range(6) for b in range(a, 6)]
SPOT = {pair: k for k, pair in enumerate(PAIRS)}


def flat(ref):
    lead, mid, lanes = ref.shape
    return ref.reshape(lead * mid, lanes)


def column(ref, fields, field, row, segment):
    return flat(ref).at[pl.ds((row * fields + field) * SEGS + segment, 8, stride=fields * SEGS), :]


def lane_of():
    return lax.broadcasted_iota(jnp.int32, (SEGS, LANES), 1)


def after(field, lane):
    turned = pltpu.roll(field, LANES - 1, 1)
    return jnp.where(lane == LANES - 1, pltpu.roll(turned, SEGS - 1, 0), turned)


def before(field, lane):
    turned = pltpu.roll(field, 1, 1)
    return jnp.where(lane == 0, pltpu.roll(turned, 1, 0), turned)


def along_columns(read, y_ref, first, last):
    lane = lane_of()

    def body(e, carry):
        u, v, w = read(e)
        at = e * 7
        for k, field in enumerate((u, v, w)):
            ahead, behind = after(field, lane), before(field, lane)
            both = ahead + behind
            y_ref[at + 2 * k] = 0.75 * field + 0.125 * both
            y_ref[at + 2 * k + 1] = 0.5 * (ahead - behind)
            if k == 2:
                y_ref[at + 6] = both - 2.0 * field
        return carry

    lax.fori_loop(first, last, body, 0, unroll=2)


def strains_at(y_ref, e):
    at = e * 7

    def three(k):
        return y_ref[at - 7 + k], y_ref[at + k], y_ref[at + 7 + k]

    def value(k):
        m, c, p = three(k)
        return 0.75 * c + 0.125 * (p + m)

    def slope(k):
        return 0.5 * (y_ref[at + 7 + k] - y_ref[at - 7 + k])

    m, c, p = three(4)
    pair = p + m
    return [
        slope(0),
        value(3) + HOOP_CURVATURE * (0.75 * c + 0.125 * pair),
        value(1) + slope(2),
        2.0 * c - pair,
        -value(6),
        y_ref[at - 7 + 5] - y_ref[at + 7 + 5],
    ]


def laminate(c_ref, e, strain):
    at = e * 21
    total = [None] * 6
    for (a, b), k in SPOT.items():
        c = c_ref[at + k]
        term = c * strain[b]
        total[a] = term if total[a] is None else total[a] + term
        if a != b:
            term = c * strain[a]
            total[b] = term if total[b] is None else total[b] + term
    return total


def forces_at(s_ref, e, lane):
    at = e * 6

    def three(k):
        return s_ref[at - 6 + k], s_ref[at + k], s_ref[at + 6 + k]

    def value(k):
        m, c, p = three(k)
        return 0.75 * c + 0.125 * (p + m)

    def slope(k):
        return 0.5 * (s_ref[at - 6 + k] - s_ref[at + 6 + k])

    def spread(here, behind, ahead):
        return here + before(behind, lane) + after(ahead, lane)

    a, b = slope(0), value(2)
    force_u = spread(0.75 * a, 0.125 * a + 0.5 * b, 0.125 * a - 0.5 * b)
    a, b = slope(2), value(1)
    force_v = spread(0.75 * a, 0.125 * a + 0.5 * b, 0.125 * a - 0.5 * b)
    m, c, p = three(3)
    a = HOOP_CURVATURE * b - ((m + p) - 2.0 * c)
    d = value(4)
    half = slope(5)
    base = 0.125 * a - d
    force_w = spread(0.75 * a + 2.0 * d, base - half, base + half)
    return force_u, force_v, force_w


def fused(
    disp_in, load_in, found_in, lay_in, stiff, w1t, wm, wl,
    res_o, adj_o, gf_o, gm_o, gl_o, trust_o,
    disp, load, found, lay, in_s, dsp, aux, ids, lod, edge_a, edge_c, got_a, got_c, y_ref, s_ref, c_ref, x_ref, l_ref, u_ref, h_ref,
    v0, v1, v2, v3, wmt, acc_m, acc_s,
    d_out, d_in, d_mid, d_in2, e_out, e_in, e_mid, e_in2, e_end, e_in3,
    g_out, g_in, g_mid, g_in2, g_end, g_in3,
    a_s, a_r, c_s, c_r, d1_s, d1_r, d2_s, d2_r, e1_s, e1_r, e2_s, e2_r, e3_s, e3_r,
    g1_s, g1_r, g2_s, g2_r, g3_s, g3_r,
):
    me_p, me_s = lax.axis_index("patch"), lax.axis_index("sub")
    count_p, count_s = lax.axis_size("patch"), lax.axis_size("sub")

    def place(dp, ds):
        return {"patch": lax.rem(me_p + dp, count_p), "sub": lax.rem(me_s + ds, count_s)}

    up, down = count_p - 1, 1
    left, right = count_s - 1, 1
    greeted = [(0, k) for k in range(1, count_s)] + [(k, 0) for k in range(1, count_p)]
    greeted += [(a, b) for a in (up, down) for b in (left, right)]
    barrier = pltpu.get_barrier_semaphore()
    for dp, ds in greeted:
        pl.semaphore_signal(barrier, inc=1, device_id=place(dp, ds), device_id_type=MESH)

    arriving = [
        pltpu.make_async_copy(source, held, in_s.at[k])
        for k, (source, held) in enumerate(((disp_in, disp), (lay_in, lay), (found_in, found), (load_in, load)))
    ]
    for copy in arriving:
        copy.start()
    for copy in arriving[:3]:
        copy.wait()

    for t in range(TILES):
        cut = pl.ds(t * LANES, LANES)
        for f in range(3):
            column(dsp, 3, f, OWN, 8 + t)[...] = disp[f, :, cut]
        column(ids, 1, 0, OWN, 8 + t)[...] = lay[:, cut].astype(jnp.float32)
    ends = ((0, pl.ds(0, LANES)), (1, pl.ds((TILES - 1) * LANES, LANES)))
    for side, cut in ends:
        for f in range(3):
            edge_a[side, f] = disp[f, :, cut]
            edge_a[side, 4 + f] = found[f, :, cut]
        edge_a[side, 3] = lay[:, cut].astype(jnp.float32)

    pl.semaphore_wait(barrier, len(greeted))

    def send(src, dst, sent, received, to):
        return pltpu.make_async_remote_copy(
            src_ref=src, dst_ref=dst, send_sem=sent, recv_sem=received, device_id=to, device_id_type=MESH
        )

    def rows_to(ref, fields, near, far, sent, received, first):
        own, n = pl.ds(OWN, TILES), (far - near) * fields
        below = send(
            ref.at[pl.ds((16 - far) * fields, n), own, :],
            ref.at[pl.ds((8 - far) * fields, n), own, :],
            sent.at[first], received.at[first], place(down, 0),
        )
        above = send(
            ref.at[pl.ds((8 + near) * fields, n), own, :],
            ref.at[pl.ds((16 + near) * fields, n), own, :],
            sent.at[first + 1], received.at[first + 1], place(up, 0),
        )
        return [below, above]

    heading = ((0, right, 1), (0, left, 0), (down, right, 1), (down, left, 0), (up, right, 1), (up, left, 0))

    def edges_to(edge, got, fields, sent, received, first):
        return [
            send(edge.at[side, fields], got.at[k, fields], sent.at[first + k], received.at[first + k], place(dp, ds))
            for k, (dp, ds, side) in reversed(list(enumerate(heading)))
        ]

    def start(copies):
        for copy in copies:
            copy.start()

    landing = ((7, 8), (0, 8), (7, 0), (0, 0), (7, 16), (0, 16))

    first_a = (
        edges_to(edge_a, got_a, pl.ds(0, 4), a_s, a_r, 2)
        + rows_to(dsp, 3, 0, 2, a_s, a_r, 0)
        + rows_to(ids, 1, 0, 1, a_s, a_r, 8)
    )
    start(first_a)
    arriving[3].wait()
    for t in range(TILES):
        cut = pl.ds(t * LANES, LANES)
        for f in range(3):
            column(aux, 3, f, OWN, 8 + t)[...] = found[f, :, cut]
            column(lod, 3, f, 0, 8 + t)[...] = load[f, :, cut]
    for k in range(3):
        wmt[k] = wm[k].T
    w1 = w1t[...].T
    wlt = wl[...].T

    def choose_row(e, carry):
        kind = ids[e].astype(jnp.int32)
        low, middle, high = (kind & 1) == 1, (kind & 2) == 2, (kind & 4) == 4
        for k, (a, b) in enumerate(PAIRS):
            p = [jnp.where(low, stiff[a, 2 * q + 1, b], stiff[a, 2 * q, b]) for q in range(4)]
            c_ref[e * 21 + k] = jnp.where(
                high, jnp.where(middle, p[3], p[2]), jnp.where(middle, p[1], p[0])
            )
        return carry

    for copy in first_a:
        copy.wait()
    second_a = (
        rows_to(aux, 3, 0, 5, a_s, a_r, 10)
        + rows_to(ids, 1, 1, 6, a_s, a_r, 12)
        + edges_to(edge_a, got_a, pl.ds(4, 3), a_s, a_r, 14)
    )
    start(second_a)
    for k, (segment, row) in enumerate(landing):
        for f in range(3):
            column(dsp, 3, f, row, segment)[...] = got_a[k, f]
        column(ids, 1, 0, row, segment)[...] = got_a[k, 3]

    lane = lane_of()
    along_columns(lambda e: [dsp[e * 3 + f] for f in range(3)], y_ref, 6, 18)

    def strain_row(r, carry):
        e = r + 7
        strain = strains_at(y_ref, e)
        for k in range(6):
            s_ref[e * 6 + k] = strain[k]
            flat(x_ref)[pl.ds(r * (SEGS * 8) + k, SEGS, stride=8), :] = strain[k]
        return carry

    lax.fori_loop(0, 10, strain_row, 0, unroll=2)
    tile_lane = lax.broadcasted_iota(jnp.int32, (8, LANES), 1)
    beside = 10 * SEGS
    packed = jnp.zeros((8, LANES), jnp.float32)
    for r in range(10):
        ends_of = jnp.where(tile_lane < 64, x_ref[r * SEGS], x_ref[r * SEGS + 7])
        turned = pltpu.roll(ends_of, 2 * r + 1, 1)
        packed = jnp.where((tile_lane == 2 * r) | (tile_lane == 2 * r + 1), turned, packed)
    x_ref[beside] = packed

    def operand(ref, at, width):
        tiles = [ref[at + q] for q in range(width // LANES)]
        return jnp.concatenate(tiles, axis=1)[:6].astype(jnp.bfloat16)

    def learn(parts):
        for at, slot, first, width in parts:
            h_ref[slot, :, pl.ds(first, width)] = jnp.tanh(
                jnp.dot(w1, operand(x_ref, at, width), preferred_element_type=jnp.float32)
            ).astype(jnp.bfloat16)
        for k in range(3):
            for at, slot, first, width in parts:
                cut = pl.ds(first, width)
                h_ref[slot + k + 1, :, cut] = jnp.tanh(
                    jnp.dot(wm[k], h_ref[slot + k, :, cut], preferred_element_type=jnp.float32)
                ).astype(jnp.bfloat16)
        for at, slot, first, width in parts:
            out = jnp.dot(wl[...], h_ref[slot + 3, :, pl.ds(first, width)], preferred_element_type=jnp.float32)
            for q in range(width // LANES):
                l_ref[at + q, 0:6, :] = out[:, q * LANES : (q + 1) * LANES]

    def row_parts(r, slot):
        return [
            (r * SEGS + 8 + c * (STEP // LANES), slot, c * STEP, STEP) for c in range(2048 // STEP)
        ]

    def stress_row(r):
        e = r + 7
        choose_row(e, 0)
        stress = laminate(c_ref, e, [s_ref[e * 6 + k] for k in range(6)])
        for k in range(6):
            s_ref[e * 6 + k] = stress[k] + flat(l_ref)[pl.ds(r * (SEGS * 8) + k, SEGS, stride=8), :]

    def residual_row(e):
        force = forces_at(s_ref, e, lane)
        for f in range(3):
            v0[e * 3 + f] = force[f] + aux[e * 3 + f] * dsp[e * 3 + f] - lod[(e - 8) * 3 + f]

    def residual_to(e):
        own, row = pl.ds(OWN, TILES), v0.at[pl.ds(e * 3, 3), pl.ds(OWN, TILES), :]
        return [
            send(row, v0.at[pl.ds((e - 8) * 3, 3), own, :], c_s.at[e - 2], c_r.at[e - 2], place(down, 0)),
            send(row, v0.at[pl.ds((e + 8) * 3, 3), own, :], c_s.at[e + 6], c_r.at[e + 6], place(up, 0)),
        ]

    learn([(beside, 32, 0, LANES)] + row_parts(0, 36))
    for r in range(10):
        turned = pltpu.roll(l_ref[beside], LANES - 1 - 2 * r, 1)
        l_ref[r * SEGS] = turned
        l_ref[r * SEGS + 7] = turned
    for r in (1, 2):
        stress_row(r - 1)
        learn(row_parts(r, (r - 1) * 4))

    def pipelined_row(r, carry):
        @pl.when(r > 3)
        def _():
            start(residual_to(r + 4))

        stress_row(r - 1)
        residual_row(r + 5)
        learn(row_parts(r, (r - 1) * 4))
        return carry

    lax.fori_loop(3, 10, pipelined_row, 0)
    start(residual_to(14))
    stress_row(9)
    residual_row(15)
    start(residual_to(15))
    for side, t in ((0, 0), (1, TILES - 1)):
        for f in range(3):
            edge_c[side, f] = column(v0, 3, f, OWN, 8 + t)[...]
    moves_c = edges_to(edge_c, got_c, pl.ds(0, 3), c_s, c_r, 0)
    start(moves_c)
    for copy in second_a:
        copy.wait()
    for k, (segment, row) in enumerate(landing):
        for f in range(3):
            column(aux, 3, f, row, segment)[...] = got_a[k, 4 + f]
    lax.fori_loop(2, 7, choose_row, 0)
    lax.fori_loop(17, 22, choose_row, 0)
    for t in range(TILES):
        for f in range(3):
            res_o[f, :, pl.ds(t * LANES, LANES)] = column(v0, 3, f, OWN, 8 + t)[...]
    for copy in moves_c:
        copy.wait()
    for e in range(8, 16):
        for copy in residual_to(e):
            copy.wait()
    for k, (segment, row) in enumerate(landing):
        for f in range(3):
            column(v0, 3, f, row, segment)[...] = got_c[k, f]

    def mean(k):
        total = stiff[k, 0, k]
        for q in range(1, 8):
            total = total + stiff[k, q, k]
        return total * 0.125

    half = 1.0 + 8.0 * jnp.maximum(mean(3), mean(4))
    center = jnp.full((1, LANES), half, jnp.float32)
    inverse = 1.0 / center

    def apply_stiffness(v, older, out, first, last):
        along_columns(lambda e: [v[e * 3 + f] for f in range(3)], y_ref, first - 2, last + 2)

        def body(e, carry):
            stress = laminate(c_ref, e, strains_at(y_ref, e))
            for k in range(6):
                s_ref[e * 6 + k] = stress[k]
            return carry

        lax.fori_loop(first - 1, last + 1, body, 0, unroll=2)

        def finish(e, carry):
            force = forces_at(s_ref, e, lane)
            for f in range(3):
                here = v[e * 3 + f]
                image = force[f] + aux[e * 3 + f] * here
                if older is None:
                    out[e * 3 + f] = inverse * image - here
                else:
                    out[e * 3 + f] = (2.0 * inverse) * image - 2.0 * here - older[e * 3 + f]
            return carry

        lax.fori_loop(first, last, finish, 0, unroll=2)

    apply_stiffness(v0, None, v1, 3, 21)
    apply_stiffness(v1, v0, v2, 5, 19)
    apply_stiffness(v2, v1, v3, 7, 17)
    along_columns(lambda e: [v3[e * 3 + f] for f in range(3)], y_ref, 7, 17)

    def folded(field):
        return field[8:16] + field[16:24]

    def sums_row(e, totals):
        strain = strains_at(y_ref, e)
        stress = laminate(c_ref, e, strain)
        energy = strain[0] * stress[0]
        for k in range(1, 6):
            energy = energy + strain[k] * stress[k]
        totals = list(totals)
        for f in range(3):
            a, b, c, d = v0[e * 3 + f], v1[e * 3 + f], v2[e * 3 + f], v3[e * 3 + f]
            energy = energy + aux[e * 3 + f] * (d * d)
            for k, product in enumerate((a * a, a * b, b * b, b * c, c * c, c * d, d * d)):
                totals[k] = totals[k] + folded(product)
        totals[7] = totals[7] + folded(energy)
        return tuple(totals)

    totals = lax.fori_loop(8, 16, sums_row, tuple(jnp.zeros((8, LANES), jnp.float32) for _ in range(8)), unroll=2)
    spots = lax.broadcasted_iota(jnp.int32, (1, LANES), 1)
    row = jnp.zeros((1, LANES), jnp.float32)
    for k, t in enumerate(totals):
        whole = jnp.sum(jnp.sum(t, axis=0, keepdims=True), axis=1, keepdims=True)
        row = jnp.where(spots == k, whole, row)
    d_out[...] = row

    def farthest_first(count):
        return sorted(range(1, count), key=lambda k: (-min(k, count - k) - 2 * (k % 2), k))

    def shared(source, slots, sent, received, count, mine, spot, piece=None):
        copies = []
        for k in farthest_first(count):
            src = source if piece is None else source.at[lax.rem(mine + k, count)]
            copies.append(send(src, slots.at[mine], sent.at[k], received.at[mine], spot(k)))
        start(copies)
        own = source if piece is None else source.at[mine]
        slots[mine] = own[...]

        def finish():
            for k in range(1, count):
                other = lax.rem(mine + k, count)
                src = source if piece is None else source.at[other]
                send(src, slots.at[other], sent.at[k], received.at[other], spot(k)).wait()

        return finish

    def summed(slots, count):
        total = slots[0]
        for k in range(1, count):
            total = total + slots[k]
        return total

    by_sub, by_patch = (lambda k: place(0, k)), (lambda k: place(k, 0))
    shared(d_out, d_in, d1_s, d1_r, count_s, me_s, by_sub)()
    d_mid[...] = summed(d_in, count_s)
    shared(d_mid, d_in2, d2_s, d2_r, count_p, me_p, by_patch)()
    everyone = summed(d_in2, count_p)
    n = [jnp.broadcast_to(everyone[:, k : k + 1], (1, LANES)) for k in range(8)]
    n34 = (2.0 * inverse) * n[7] - 2.0 * n[6] - n[5]
    m = [n[0], n[1]]
    for k in (2, 3, 4, 5, 6):
        m.append(2.0 * n[k] - m[k % 2])
    m.append(2.0 * n34 - m[1])

    def gram(i, j):
        return 0.5 * (m[i + j] + m[abs(i - j)])

    def form(x, y):
        total, size = None, None
        for i, a in enumerate(x):
            for j, b in enumerate(y):
                term = a * b * gram(i, j)
                total = term if total is None else total + term
                size = jnp.abs(term) if size is None else size + jnp.abs(term)
        return total, size / total

    def image_of(x):
        zero = jnp.zeros((1, LANES), jnp.float32)
        out = [center * a for a in x] + [zero]
        for j, a in enumerate(x):
            if j == 0:
                out[1] = out[1] + center * a
            else:
                out[j + 1] = out[j + 1] + (0.5 * center) * a
                out[j - 1] = out[j - 1] + (0.5 * center) * a
        return out

    one = jnp.ones((1, LANES), jnp.float32)
    zero = jnp.zeros((1, LANES), jnp.float32)
    rest, way, found_y, norm = [one], [one], [zero] * 4, m[0]
    worst = one
    for step in range(ITERS):
        image = image_of(way)
        curved, spread = form(way, image)
        worst = jnp.where(spread <= TRUST, worst, 2.0 * TRUST * one)
        alpha = norm / curved
        found_y = [found_y[k] + alpha * way[k] if k < len(way) else found_y[k] for k in range(4)]
        if step + 1 < ITERS:
            rest = [(rest[k] if k < len(rest) else zero) - alpha * image[k] for k in range(len(image))]
            fresh, spread = form(rest, rest)
            worst = jnp.where(spread <= TRUST, worst, 2.0 * TRUST * one)
            beta = fresh / norm
            way = [rest[k] + (beta * way[k] if k < len(way) else zero) for k in range(len(rest))]
            norm = fresh
    trust_o[0, 0] = worst[0, 0]

    def adjoint_row(e, carry):
        for f in range(3):
            at = e * 3 + f
            v0[at] = found_y[0] * v0[at] + found_y[1] * v1[at] + found_y[2] * v2[at] + found_y[3] * v3[at]
        return carry

    lax.fori_loop(7, 17, adjoint_row, 0, unroll=2)
    for t in range(TILES):
        for f in range(3):
            adj_o[f, :, pl.ds(t * LANES, LANES)] = column(v0, 3, f, OWN, 8 + t)[...]
    along_columns(lambda e: [v0[e * 3 + f] for f in range(3)], y_ref, 7, 17)

    def upstream_row(e, carry):
        strain = strains_at(y_ref, e)
        for k in range(6):
            flat(u_ref)[pl.ds((e - 8) * (SEGS * 8) + k, SEGS, stride=8), :] = strain[k]
        return carry

    lax.fori_loop(8, 16, upstream_row, 0, unroll=2)

    acc_m[...] = jnp.zeros_like(acc_m)
    acc_s[...] = jnp.zeros_like(acc_s)

    def derive(weights, signal_of, slot):
        for c in range(2048 // STEP):
            cut = pl.ds(c * STEP, STEP)
            h = h_ref[slot, :, cut].astype(jnp.float32)
            signal = jnp.dot(weights, signal_of(c, cut), preferred_element_type=jnp.float32)
            h_ref[slot, :, cut] = (signal * (1.0 - jnp.square(h))).astype(jnp.bfloat16)

    def back_last(r, carry):
        slot = r * 4 + 3
        u = operand(u_ref, r * SEGS + 8, 2048)
        acc_s[0:6] += outer_product(u, h_ref[slot])
        derive(wlt, lambda c, cut: u[:, c * STEP : (c + 1) * STEP], slot)
        return carry

    def back_mid(k):
        def body(r, carry):
            slot = r * 4 + k
            acc_m[k] += outer_product(h_ref[slot + 1], h_ref[slot])
            derive(wmt[k], lambda c, cut: h_ref[slot + 1, :, cut], slot)
            return carry

        lax.fori_loop(0, 8, body, 0)

    def back_first(r, carry):
        acc_s[8:14] += outer_product(operand(x_ref, (r + 1) * SEGS + 8, 2048), h_ref[r * 4])
        return carry

    lax.fori_loop(0, 8, back_last, 0)
    back_mid(2)
    back_mid(1)
    for k in range(16):
        e_out[k, 0:8, :] = acc_m[1, 8 * k : 8 * k + 8]
        e_out[k, 8:16, :] = acc_m[2, 8 * k : 8 * k + 8]
    finish_e1 = shared(e_out, e_in, e1_s, e1_r, count_s, me_s, by_sub, piece=True)
    back_mid(0)
    lax.fori_loop(0, 8, back_first, 0, unroll=2)
    for k in range(16):
        g_out[k, 0:8, :] = acc_m[0, 8 * k : 8 * k + 8]
        g_out[k, 8:9, :] = acc_s[k : k + 1]
    finish_g1 = shared(g_out, g_in, g1_s, g1_r, count_s, me_s, by_sub, piece=True)
    finish_e1()
    e_mid[...] = summed(e_in, count_s)
    finish_e2 = shared(e_mid, e_in2, e2_s, e2_r, count_p, me_p, by_patch)
    finish_g1()
    g_mid[...] = summed(g_in, count_s)
    finish_g2 = shared(g_mid, g_in2, g2_s, g2_r, count_p, me_p, by_patch)
    finish_e2()
    e_end[...] = summed(e_in2, count_p)
    finish_e3 = shared(e_end, e_in3, e3_s, e3_r, count_s, me_s, by_sub)
    finish_g2()
    g_end[...] = summed(g_in2, count_p)
    finish_g3 = shared(g_end, g_in3, g3_s, g3_r, count_s, me_s, by_sub)
    finish_e3()
    for k in range(16):
        gm_o[1, 8 * k : 8 * k + 8] = e_in3[k, 0:8, :]
        gm_o[2, 8 * k : 8 * k + 8] = e_in3[k, 8:16, :]
    finish_g3()
    for k in range(16):
        gm_o[0, 8 * k : 8 * k + 8] = g_in3[k, 0:8, :]
    for k in range(6):
        gl_o[k : k + 1] = g_in3[k, 8:9, :]
        gf_o[k : k + 1] = g_in3[8 + k, 8:9, :]


def per_device(displacement, load, foundation, layup, layup_stiffness, w_first, w_mid, w_last):
    vmem = pl.BlockSpec(memory_space=pltpu.VMEM)
    smem = pl.BlockSpec(memory_space=pltpu.SMEM)
    f32, bf16 = jnp.float32, jnp.bfloat16

    def rows(fields, count=ROWS):
        return pltpu.VMEM((count * fields, SEGS, LANES), f32)

    dma = pltpu.SemaphoreType.DMA
    out = pl.pallas_call(
        fused,
        out_shape=[
            jax.ShapeDtypeStruct(displacement.shape, f32),
            jax.ShapeDtypeStruct(displacement.shape, f32),
            jax.ShapeDtypeStruct((6, 128), f32),
            jax.ShapeDtypeStruct((3, 128, 128), f32),
            jax.ShapeDtypeStruct((6, 128), f32),
            jax.ShapeDtypeStruct((1, 1), f32),
        ],
        in_specs=[pl.BlockSpec(memory_space=pl.ANY)] * 4 + [smem] + [vmem] * 3,
        out_specs=[vmem] * 5 + [smem],
        scratch_shapes=[
            pltpu.VMEM(displacement.shape, f32), pltpu.VMEM(displacement.shape, f32),
            pltpu.VMEM(displacement.shape, f32), pltpu.VMEM(layup.shape, jnp.int32), dma((4,)),
            rows(3), rows(3), rows(1), rows(3, 8),
            pltpu.VMEM((2, 7, 8, LANES), f32), pltpu.VMEM((2, 3, 8, LANES), f32),
            pltpu.VMEM((6, 7, 8, LANES), f32), pltpu.VMEM((6, 3, 8, LANES), f32),
            rows(7), rows(6), rows(21),
            pltpu.VMEM((11 * SEGS, 8, LANES), f32),
            pltpu.VMEM((11 * SEGS, 8, LANES), f32),
            pltpu.VMEM((8 * SEGS, 8, LANES), f32),
            pltpu.VMEM((10 * 4, 128, 2048), bf16),
            rows(3), rows(3), rows(3), rows(3),
            pltpu.VMEM((3, 128, 128), bf16),
            pltpu.VMEM((3, 128, 128), f32), pltpu.VMEM((16, 128), f32),
            pltpu.VMEM((1, LANES), f32), pltpu.VMEM((16, 1, LANES), f32),
            pltpu.VMEM((1, LANES), f32), pltpu.VMEM((16, 1, LANES), f32),
        ] + [
            pltpu.VMEM(shape, f32)
            for n in (16, 9)
            for shape in [(16, n, LANES), (16, n, LANES), (n, LANES)] + [(16, n, LANES), (n, LANES), (16, n, LANES)]
        ] + [
            dma((20,)), dma((20,)), dma((22,)), dma((22,)),
        ] + [dma((16,)) for _ in range(16)],
        compiler_params=pltpu.CompilerParams(
            collective_id=0, has_side_effects=True, vmem_limit_bytes=46 << 20
        ),
        name="adjoint_step",
    )(
        displacement, load, foundation, layup, layup_stiffness.transpose(1, 0, 2), w_first.T, w_mid, w_last
    )
    fast, trust = (out[0], out[1], out[2].T, out[3], out[4]), out[5][0, 0]
    operands = (displacement, load, foundation, layup, layup_stiffness, w_first, w_mid, w_last)
    return lax.cond(trust <= TRUST, lambda: fast, lambda: careful(*operands))


def solution(mesh):
    return jax.shard_map(
        per_device,
        mesh=mesh,
        in_specs=(
            P(None, "patch", "sub"),
            P(None, "patch", "sub"),
            P(None, "patch", "sub"),
            P("patch", "sub"),
            P(),
            P(),
            P(),
            P(),
        ),
        out_specs=(P(None, "patch", "sub"), P(None, "patch", "sub"), P(), P(), P()),
        check_vma=False,
    )
```
